256 devices in a mesh: ctx: 16 (over z, core), exp: 16 (over x, y).
Axes of the slice: x: 4, y: 4, z: 8, core: 2. Of those that a mesh axis runs over, the one named last changes fastest.
Arguments:
- queries: bfloat16 [2, 16384, 2560], P(None, ('ctx', 'exp'))
- key_states: bfloat16 [2, 16384, 512], P(None, ('ctx', 'exp'))
- value_state_rows: bfloat16 [2, 16384, 512], P(None, ('ctx', 'exp')), may hold values from -6 to 6
- block_lists: int32 [32], replicated, may hold values from 0 to 31, as said below
- hidden: bfloat16 [8192, 5120], P(('ctx', 'exp')), may hold values from -8 to 8
- router: bfloat16 [5120, 16], replicated, may hold values from -0.078125 to 0.078125
- expert_ids: int32 [8192, 1], P(('ctx', 'exp')), may hold values from 0 to 15; in each aligned block of 32 rows (0 to 31, 32 to 63, ...) at most 4 rows name the same one
- w_gate: bfloat16 [16, 5120, 4096], P('exp', None, 'ctx'), may hold values from -0.078125 to 0.078125
- w_up: bfloat16 [16, 5120, 4096], P('exp', None, 'ctx'), may hold values from -0.078125 to 0.078125
- w_down: bfloat16 [16, 4096, 5120], P('exp', 'ctx'), may hold values from -0.1875 to 0.1875
Outputs:
- attention: bfloat16 [2, 16384, 2560], P(None, ('ctx', 'exp'))
- moe_out: bfloat16 [8192, 5120], P(('ctx', 'exp'))
The draws below stay inside these ranges and needn't reach their ends.
Inputs may be any that keep to these rules, and one draw needn't show every extreme that they name: block_lists[b] is a block before b, or b itself when block b attends only to its own keys (always for b = 0 and for b = 31). Block p is held by index min(p, 31 - p) of ctx; for each d < 16 with block_lists[d] != d and block_lists[31 - d] != 31 - d, the two listed blocks are held by different indices. `expert_ids`: among the rows of one device no expert is named more than 4 times.
All inputs are finite; a program needn't handle non-finite values.
Results may differ from the reference program's by a relative error of at most 0.023.
Values may be sent and summed in bfloat16 or wider, within the bound.
No kernel may reach another device: no remote copies, remote signals or barrier semaphores. Data moves between devices by JAX's collectives and lax.ppermute only.
A program may use at most 128 MiB of HBM per device.

```python
import math
import jax
import jax.numpy as jnp
import numpy as np
from jax import lax

MODEL_DIM = 5120
QUERY_HEADS = 20
KEY_HEADS = 4
HEAD_DIM = 128
HIDDEN_PER_SHARD = 256
MOE_DEV = 32
HID = 4096
EXPERTS = 16
KEY_BLOCK_SIZE = 1024
NBLK = 32
HALF_TOKENS = 16384
CAP = 4
MOE_TOKENS = 8192
SLOT_COUNT = 1024
N_CTX = 16
N_EXP = 16


def key_matrix_full(key):
    starting_keys = jax.random.normal(jax.random.fold_in(key, 101), (2, HALF_TOKENS, KEY_HEADS * HEAD_DIM), jnp.float32)
    return starting_keys


def draw_key_states(key, part):
    return key_matrix_full(key).astype(jnp.bfloat16)


def draw_queries(key, part):
    drawn = jax.random.normal(jax.random.fold_in(key, 103), (2, HALF_TOKENS, QUERY_HEADS * HEAD_DIM), jnp.float32)
    return drawn.astype(jnp.bfloat16)


def draw_block_lists(key, part):
    half_count = NBLK // 2
    block_number_index = jnp.arange(NBLK, dtype=jnp.int32)
    preceding_blocks = jax.random.randint(jax.random.fold_in(key, 201), (NBLK,), 0, jnp.maximum(block_number_index, 1))
    favored = jax.random.randint(jax.random.fold_in(key, 202), (), 0, max(NBLK // 4, 1))
    coin_flip = jax.random.randint(jax.random.fold_in(key, 203), (NBLK,), 0, 2)
    picked = jnp.where((coin_flip == 0) & (favored < block_number_index), favored, preceding_blocks)
    vacant = jax.random.randint(jax.random.fold_in(key, 204), (NBLK,), 0, 8) == 0
    vacant = vacant | (block_number_index == 0) | (block_number_index == NBLK - 1)
    picked = jnp.where(vacant, block_number_index, picked)
    front_list = picked[:half_count]
    back_list = picked[half_count:][::-1]
    target = jnp.arange(half_count, dtype=jnp.int32)
    front_owner = jnp.minimum(front_list, NBLK - 1 - front_list)
    back_owner = jnp.minimum(back_list, NBLK - 1 - back_list)
    clash = (front_list != target) & (back_list != NBLK - 1 - target) & (front_owner == back_owner)
    back_list = jnp.where(clash, NBLK - 2 - target, back_list)
    return jnp.concatenate([front_list, back_list[::-1]]).astype(jnp.int32)


def block_scale(rng, shape, shards, least, top_value):
    level = 1.0
    for dim, blocks in shards:
        heights = jax.random.uniform(jax.random.fold_in(jax.random.fold_in(rng, 6), dim), (blocks,), jnp.float32, least / len(shards), top_value / len(shards))
        level = level * jnp.repeat(jnp.exp(heights), shape[dim] // blocks).reshape((-1,) + (1,) * (len(shape) - 1 - dim))
    return level


def shared_out(own_key, own, number, rows, number_of, top, limit, slope):
    order = jax.random.permutation(own_key, number_of)
    packed, ordinary = shares(number_of, rows * top, limit, slope, True), shares(number_of, rows * top, limit, slope, False)
    places = jnp.arange(number_of)

    def named(sizes, turn):
        used = int((sizes > 0).sum())
        fixed = max(1, used // 4)
        passed = fixed + (places - fixed + turn * (used - fixed)) % max(1, number_of - fixed)
        return jnp.zeros((number_of,), jnp.int32).at[order[jnp.where(places < fixed, places, passed)]].set(jnp.asarray(sizes, jnp.int32))

    sizes = jnp.where(number % 4 == 0, named(packed, number // 4), named(ordinary, number - number // 4 - 1))
    mixed = jax.random.permutation(jax.random.fold_in(own, 3), number_of)
    giver, taker = mixed[0:number_of // 2 * 2:2], mixed[1:number_of // 2 * 2:2]
    margin = jnp.minimum(sizes[giver] - 1, limit - sizes[taker]) // 2
    margin = jnp.where((giver == order[0]) | (taker == order[0]) | (sizes[taker] == 0), 0, jnp.maximum(margin, 0))
    passed = jax.random.randint(jax.random.fold_in(own, 4), (number_of // 2,), 0, 1 << 20) % (margin + 1)
    sizes = sizes.at[giver].add(-passed).at[taker].add(passed)
    items = jnp.searchsorted(jnp.cumsum(sizes), jnp.arange(rows * top), side="right").astype(jnp.int32)
    grid = items.reshape(top, rows).T
    grid = grid[jax.random.permutation(jax.random.fold_in(own, 1), rows)]
    turn = jax.random.randint(jax.random.fold_in(own, 2), (rows, 1), 0, top)
    return jnp.take_along_axis(grid, (jnp.arange(top)[None, :] + turn) % top, axis=1)


def shares(count, total, bound, slope, full):
    loads = [(1 << 20) // math.isqrt(rank ** slope) + 1 for rank in range(1, count + 1)]
    largest = bound if full else min(bound, max(-(-total // count), total * loads[0] // sum(loads)))
    least = 1 if total - largest >= count - 1 else 0
    holding, spare = [largest] + [least] * (count - 1), total - largest - least * (count - 1)
    while spare > 0:
        movable = [i for i in range(1, count) if holding[i] < largest] or [i for i in range(1, count) if holding[i] < bound]
        mass, budget = sum([loads[i] for i in movable]), spare
        for i in movable:
            more = min(bound - holding[i], max(1, budget * loads[i] // mass), spare)
            holding[i] = holding[i] + more
            spare = spare - more
    return np.array(holding)


def normal_values(key, shape, spread, bound, pieces=(), kind=jnp.bfloat16):
    values = spread * jax.random.normal(key, shape, jnp.float32)
    if pieces:
        values = values * block_scale(key, shape, pieces, -0.22, 0.18)
    return jnp.clip(values, -bound, bound).astype(kind)


def setup_inputs(seed: int = 0) -> dict:
    splits = jax.random.split(jax.random.key(seed), 11)
    queries = draw_queries(jax.random.fold_in(splits[10], 71), 0)
    key_states = draw_key_states(jax.random.fold_in(splits[10], 71), 0)
    value_state_rows = normal_values(splits[2], (2, HALF_TOKENS, KEY_HEADS * HEAD_DIM), 1.0, 6.0, ((1, 256),))
    block_lists = draw_block_lists(jax.random.fold_in(splits[10], 71), 0)
    hidden = normal_values(splits[4], (MOE_TOKENS, MODEL_DIM), 1.5, 8.0, ((0, 256),))
    router = normal_values(splits[5], (MODEL_DIM, EXPERTS), MODEL_DIM ** -0.5, 0.078125)
    expert_ids_keys = jax.random.split(jax.random.fold_in(splits[6], 1), MOE_TOKENS // MOE_DEV)
    expert_ids_turns = jax.random.permutation(jax.random.fold_in(splits[6], 3), MOE_TOKENS // MOE_DEV)
    expert_ids = jax.vmap(lambda own, number: shared_out(jax.random.fold_in(splits[6], 2), own, number, MOE_DEV, EXPERTS, 1, CAP, 2))(expert_ids_keys, expert_ids_turns).reshape((MOE_TOKENS, 1))
    w_gate = normal_values(splits[7], (EXPERTS, MODEL_DIM, HID), MODEL_DIM ** -0.5, 0.078125, ((0, 16), (2, 16)))
    w_up = normal_values(splits[8], (EXPERTS, MODEL_DIM, HID), MODEL_DIM ** -0.5, 0.078125, ((0, 16), (2, 16)))
    w_down = normal_values(splits[9], (EXPERTS, HID, MODEL_DIM), (HID // 4) ** -0.5, 0.1875, ((0, 16), (1, 16)))
    return {"queries": queries, "key_states": key_states, "value_state_rows": value_state_rows, "block_lists": block_lists, "hidden": hidden, "router": router, "expert_ids": expert_ids, "w_gate": w_gate, "w_up": w_up, "w_down": w_down}


NEGATIVE_LARGE = -1e30


def to_blocks(stored):
    row_width = stored.shape[-1]
    second = stored[1].reshape(N_CTX, KEY_BLOCK_SIZE, row_width)[::-1]
    return jnp.concatenate([stored[0].reshape(N_CTX, KEY_BLOCK_SIZE, row_width), second], axis=0)


def from_blocks(stored):
    row_width = stored.shape[-1]
    first_half = stored[:N_CTX].reshape(HALF_TOKENS, row_width)
    second = stored[N_CTX:][::-1].reshape(HALF_TOKENS, row_width)
    return jnp.stack([first_half, second])


def reference(queries, key_states, value_state_rows, block_lists, hidden, router, expert_ids, w_gate, w_up, w_down):
    query_group_width = QUERY_HEADS // KEY_HEADS
    query_block_list = to_blocks(queries)
    key_blocks = to_blocks(key_states)
    value_blocks = to_blocks(value_state_rows)
    positions = jnp.arange(KEY_BLOCK_SIZE)

    def one_block(block_number_index):
        listed = block_lists[block_number_index]
        query_row_matrix = query_block_list[block_number_index].reshape(KEY_BLOCK_SIZE, KEY_HEADS, query_group_width, HEAD_DIM).astype(jnp.float32)
        key_block_matrix = jnp.concatenate([key_blocks[block_number_index], key_blocks[listed]], axis=0)
        key_block_matrix = key_block_matrix.reshape(2 * KEY_BLOCK_SIZE, KEY_HEADS, HEAD_DIM).astype(jnp.float32)
        value_row_matrix = jnp.concatenate([value_blocks[block_number_index], value_blocks[listed]], axis=0)
        value_row_matrix = value_row_matrix.reshape(2 * KEY_BLOCK_SIZE, KEY_HEADS, HEAD_DIM).astype(jnp.float32)
        scores = jnp.einsum("qhgd,khd->hgqk", query_row_matrix, key_block_matrix) * (HEAD_DIM ** -0.5)
        causal = positions[None, :] <= positions[:, None]
        listed_ok = jnp.broadcast_to(listed != block_number_index, (KEY_BLOCK_SIZE, KEY_BLOCK_SIZE))
        allowed = jnp.concatenate([causal, listed_ok], axis=1)
        masked = jnp.where(allowed, scores, NEGATIVE_LARGE)
        row_peak = jnp.max(masked, axis=-1, keepdims=True)
        weights = jnp.where(allowed, jnp.exp(masked - row_peak), 0.0)
        row_total = jnp.sum(weights, axis=-1)
        rounded = lax.optimization_barrier(weights.astype(jnp.bfloat16)).astype(jnp.float32)
        mixed_rows = jnp.einsum("hgqk,khd->qhgd", rounded, value_row_matrix)
        mixed_rows = mixed_rows / jnp.transpose(row_total, (2, 0, 1))[..., None]
        return mixed_rows.reshape(KEY_BLOCK_SIZE, QUERY_HEADS * HEAD_DIM).astype(jnp.bfloat16)

    attention = from_blocks(lax.map(one_block, jnp.arange(NBLK)))

    expert_table = router.shape[1]
    logits = jnp.dot(hidden, router, preferred_element_type=jnp.float32)
    selected_expert = expert_ids[:, 0]
    onehot = (selected_expert[:, None] == jnp.arange(expert_table)[None, :]).astype(jnp.float32)
    gate_score = jax.nn.sigmoid(jnp.sum(logits * onehot, axis=1))
    scaled_scores = (hidden.astype(jnp.float32) * gate_score[:, None]).astype(jnp.bfloat16)
    devices = N_CTX * N_EXP
    per_device = onehot.reshape(devices, MOE_DEV, expert_table)
    slot_rank = (jnp.sum(jnp.cumsum(per_device, axis=1) * per_device, axis=-1) - 1.0).reshape(MOE_TOKENS).astype(jnp.int32)
    source = jnp.arange(MOE_TOKENS, dtype=jnp.int32) // MOE_DEV
    slot_position_index = source * CAP + slot_rank
    holding_array = jnp.zeros((expert_table, SLOT_COUNT, MODEL_DIM), jnp.bfloat16).at[selected_expert, slot_position_index].set(scaled_scores)

    def run_expert(operands):
        tokens, gate_weight, up_weight, down_weight = operands
        gate_out = jnp.dot(tokens, gate_weight, preferred_element_type=jnp.float32)
        up_out = jnp.dot(tokens, up_weight, preferred_element_type=jnp.float32)
        hidden_activation = (jax.nn.silu(gate_out) * up_out).astype(jnp.bfloat16)
        portions = jnp.transpose(hidden_activation.reshape(SLOT_COUNT, N_CTX, HIDDEN_PER_SHARD), (1, 0, 2))
        down_portions = down_weight.reshape(N_CTX, HIDDEN_PER_SHARD, MODEL_DIM)

        def append_portion(running, operand_pair):
            act_piece, down_piece = operand_pair
            partial_value = jnp.dot(act_piece, down_piece, preferred_element_type=jnp.float32).astype(jnp.bfloat16)
            partial_value = lax.optimization_barrier(partial_value).astype(jnp.float32)
            return running + partial_value, None

        summed_output = lax.scan(append_portion, jnp.zeros((SLOT_COUNT, MODEL_DIM), jnp.float32), (portions, down_portions))[0]
        return summed_output.astype(jnp.bfloat16)

    results = lax.map(run_expert, (holding_array, w_gate, w_up, w_down))
    moe_out = results[selected_expert, slot_position_index]
    return attention, moe_out
```

```python
import jax
import jax.numpy as jnp
from jax import lax
from jax.experimental import pallas as pl
from jax.experimental.pallas import tpu as pltpu
from jax.sharding import PartitionSpec as P

HEAD_DIM = 128
NEGATIVE_LARGE = -1e30
SIDE = 4
RINGS = [[2 * z + c for z in range(8)] for c in range(2)]
CORE_SWAP = [(i, i ^ 1) for i in range(16)]


def shift_x(d):
    return [(4 * a + b, 4 * ((a + d) % 4) + b) for a in range(4) for b in range(4)]


def shift_y(d):
    return [(4 * a + b, 4 * a + (b + d) % 4) for a in range(4) for b in range(4)]


def ordinary(vmem=48):
    return pltpu.CompilerParams(
        dimension_semantics=("arbitrary",), vmem_limit_bytes=vmem * 1024 * 1024
    )


def pick_kernel(table, source, *outs):
    x = table[4]
    for d in range(SIDE):
        h = lax.rem(x + d, SIDE)
        outs[d][0] = source[0, :, pl.ds(pl.multiple_of(h * 256, 256), 256)]


def pick_heads(everyone, table):
    rows, width = everyone.shape[1], everyone.shape[2]
    part = jax.ShapeDtypeStruct((4, rows, 256), everyone.dtype)
    return pl.pallas_call(
        pick_kernel,
        grid_spec=pltpu.PrefetchScalarGridSpec(
            num_scalar_prefetch=1,
            grid=(4,),
            in_specs=[pl.BlockSpec((1, rows, width), lambda i, t: (t[i], 0, 0))],
            out_specs=[pl.BlockSpec((1, rows, 256), lambda i, t: (i, 0, 0))] * SIDE,
        ),
        out_shape=[part] * SIDE,
        compiler_params=ordinary(16),
        cost_estimate=pl.CostEstimate(flops=0, bytes_accessed=2 << 20, transcendentals=0),
        name="pick_heads",
    )(table, everyone)


def split_kernel(where, source, *outs):
    x = where[0]
    width = outs[0].shape[2]
    for d in range(SIDE):
        h = lax.rem(x + d, SIDE)
        outs[d][...] = source[:, :, pl.ds(pl.multiple_of(h * width, 128), width)]


def split_queries(queries, where):
    part = jax.ShapeDtypeStruct(queries.shape[:2] + (queries.shape[2] // SIDE,), queries.dtype)
    return pl.pallas_call(
        split_kernel,
        grid_spec=pltpu.PrefetchScalarGridSpec(
            num_scalar_prefetch=1,
            grid=(1,),
            in_specs=[pl.BlockSpec(queries.shape, lambda i, t: (0, 0, 0))],
            out_specs=[pl.BlockSpec(part.shape, lambda i, t: (0, 0, 0))] * SIDE,
        ),
        out_shape=[part] * SIDE,
        compiler_params=ordinary(16),
        cost_estimate=pl.CostEstimate(flops=0, bytes_accessed=1310720, transcendentals=0),
        name="split_queries",
    )(where, queries)


def stack_kernel(where, *refs):
    x = where[0]
    out = refs[SIDE]
    for d in range(SIDE):
        out[lax.rem(x + SIDE - d, SIDE)] = refs[d][...]


def stack_sources(parts, where):
    shape = parts[0].shape
    zeros = (0,) * len(shape)
    return pl.pallas_call(
        stack_kernel,
        grid_spec=pltpu.PrefetchScalarGridSpec(
            num_scalar_prefetch=1,
            grid=(1,),
            in_specs=[pl.BlockSpec(shape, lambda i, t: zeros)] * SIDE,
            out_specs=pl.BlockSpec((SIDE,) + shape, lambda i, t: (0,) + zeros),
        ),
        out_shape=jax.ShapeDtypeStruct((SIDE,) + shape, parts[0].dtype),
        compiler_params=ordinary(16),
        cost_estimate=pl.CostEstimate(flops=0, bytes_accessed=1 << 20, transcendentals=0),
        name="stack_sources",
    )(where, *parts)


def join_kernel(where, *refs):
    x = where[0]
    out = refs[SIDE]
    width = refs[0].shape[2]
    for d in range(SIDE):
        h = lax.rem(x + d, SIDE)
        out[:, :, pl.ds(pl.multiple_of(h * width, 128), width)] = refs[d][...]


def join_heads(parts, where):
    shape = parts[0].shape
    full = shape[:2] + (shape[2] * SIDE,)
    return pl.pallas_call(
        join_kernel,
        grid_spec=pltpu.PrefetchScalarGridSpec(
            num_scalar_prefetch=1,
            grid=(1,),
            in_specs=[pl.BlockSpec(shape, lambda i, t: (0, 0, 0))] * SIDE,
            out_specs=pl.BlockSpec(full, lambda i, t: (0, 0, 0)),
        ),
        out_shape=jax.ShapeDtypeStruct(full, parts[0].dtype),
        compiler_params=ordinary(16),
        cost_estimate=pl.CostEstimate(flops=0, bytes_accessed=1310720, transcendentals=0),
        name="join_heads",
    )(where, *parts)


NT = (((1,), (1,)), ((), ()))


def attend_kernel(where, q0, q1, q2, q3, r0, r1, r2, r3a, r3b, o0, o1, o2, o3, kown, vown, klist, vlist, qall, oall):
    p = pl.program_id(0)
    x, y, usable = where[0], where[1], where[2 + p]
    pieces = (r0, r1, r2)
    for xs in range(SIDE):
        last = r3a if xs < 2 else r3b
        for turn in range(SIDE):
            piece = pieces[turn][xs] if turn < 3 else last[xs % 2]
            at = pl.ds(xs * 256 + turn * 64, 64)
            kown[at, :] = piece[0, 0, :, :HEAD_DIM]
            vown[at, :] = piece[0, 0, :, HEAD_DIM:]
            klist[at, :] = piece[1, 0, :, :HEAD_DIM]
            vlist[at, :] = piece[1, 0, :, HEAD_DIM:]
    scaling = HEAD_DIM ** (-0.5)
    group = q0.shape[2] // HEAD_DIM
    rows = 64 * group
    qs, outs = (q0, q1, q2, q3), (o0, o1, o2, o3)
    query_row = lax.rem(lax.broadcasted_iota(jnp.int32, (rows, 256), 0), 64)
    key_index = lax.broadcasted_iota(jnp.int32, (rows, 256), 1)
    turn = key_index // 64
    behind = jnp.where(turn == 0, 0, jnp.where(turn == 1, 3, jnp.where(turn == 2, 1, 2)))
    key_pos = lax.rem(y + behind, SIDE) * 64 + lax.rem(key_index, 64)
    diagonal = key_pos <= y * 64 + query_row
    for d in range(SIDE):
        qall[lax.rem(x + SIDE - d, SIDE)] = qs[d][0]
    for case in range(SIDE):
        query = jnp.concatenate(
            [qall[case, :, g * HEAD_DIM : (g + 1) * HEAD_DIM] for g in range(group)], axis=0
        )
        before = case * 256
        own = lax.dot_general(
            query, kown[pl.ds(before, 256), :], NT, preferred_element_type=jnp.float32
        )
        own = jnp.where(diagonal, own * scaling, NEGATIVE_LARGE)
        far = lax.dot_general(query, klist[...], NT, preferred_element_type=jnp.float32)
        far = jnp.where(usable > 0, far * scaling, NEGATIVE_LARGE)
        top = jnp.maximum(jnp.max(own, axis=1, keepdims=True), jnp.max(far, axis=1, keepdims=True))
        if case:
            near = lax.dot_general(
                query, kown[pl.ds(0, before), :], NT, preferred_element_type=jnp.float32
            )
            near = near * scaling
            top = jnp.maximum(top, jnp.max(near, axis=1, keepdims=True))
        own = jnp.exp(own - top)
        far = jnp.exp(far - top)
        total = jnp.sum(own, axis=1, keepdims=True) + jnp.sum(far, axis=1, keepdims=True)
        mixed = jnp.dot(
            own.astype(jnp.bfloat16), vown[pl.ds(before, 256), :], preferred_element_type=jnp.float32
        ) + jnp.dot(far.astype(jnp.bfloat16), vlist[...], preferred_element_type=jnp.float32)
        if case:
            near = jnp.exp(near - top)
            total = total + jnp.sum(near, axis=1, keepdims=True)
            mixed = mixed + jnp.dot(
                near.astype(jnp.bfloat16),
                vown[pl.ds(0, before), :],
                preferred_element_type=jnp.float32,
            )
        mixed = (mixed / total).astype(jnp.bfloat16)
        for g in range(group):
            oall[case, :, g * HEAD_DIM : (g + 1) * HEAD_DIM] = mixed[g * 64 : (g + 1) * 64]
    for d in range(SIDE):
        outs[d][0] = oall[lax.rem(x + SIDE - d, SIDE)]


def attend(where, qs, rs):
    qspec = pl.BlockSpec((1,) + qs[0].shape[1:], lambda i, t: (i, 0, 0))

    def rspec(r):
        return pl.BlockSpec((r.shape[0], 2, 1) + r.shape[3:], lambda i, t: (0, 0, i, 0, 0))

    return pl.pallas_call(
        attend_kernel,
        grid_spec=pltpu.PrefetchScalarGridSpec(
            num_scalar_prefetch=1,
            grid=(2,),
            in_specs=[qspec] * SIDE + [rspec(r) for r in rs],
            out_specs=[qspec] * SIDE,
            scratch_shapes=[pltpu.VMEM((1024, HEAD_DIM), jnp.bfloat16)] * 4
            + [pltpu.VMEM((SIDE,) + qs[0].shape[1:], jnp.bfloat16)] * 2,
        ),
        out_shape=[jax.ShapeDtypeStruct(q.shape, q.dtype) for q in qs],
        compiler_params=ordinary(40),
        cost_estimate=pl.CostEstimate(
            flops=2200000000, bytes_accessed=4 << 20, transcendentals=4300000
        ),
        name="attend",
    )(where, *qs, *rs)


def attend_all(queries, key_states, value_state_rows, block_lists):
    ctx_count = lax.axis_size("ctx")
    blocks_total = 2 * ctx_count
    ctx_index = lax.axis_index("ctx")
    exp_index = lax.axis_index("exp")
    x, y = exp_index // SIDE, exp_index % SIDE
    where = jnp.stack([x, y]).astype(jnp.int32)
    heads = key_states.shape[2] // HEAD_DIM
    columns = []
    for h in range(heads):
        columns.append(key_states[:, :, h * HEAD_DIM : (h + 1) * HEAD_DIM])
        columns.append(value_state_rows[:, :, h * HEAD_DIM : (h + 1) * HEAD_DIM])
    paired = jnp.concatenate(columns, axis=2)
    everyone = lax.all_gather(paired, "ctx", axis=0, tiled=True)
    own_blocks = jnp.stack([ctx_index, blocks_total - 1 - ctx_index])
    listed = block_lists[own_blocks]
    usable = (listed != own_blocks).astype(jnp.int32)
    wanted = jnp.concatenate([own_blocks, listed])
    holder = jnp.minimum(wanted, blocks_total - 1 - wanted)
    row = 2 * holder + (wanted >= ctx_count).astype(jnp.int32)
    table = jnp.concatenate([row, x[None]]).astype(jnp.int32)

    mine = split_queries(queries, where)
    qs = [mine[0]] + [lax.ppermute(mine[d], "exp", shift_x(d)) for d in range(1, SIDE)]
    picked = pick_heads(everyone, table)
    received = [picked[0]] + [lax.ppermute(picked[d], "exp", shift_x(d)) for d in range(1, SIDE)]
    r0 = stack_sources(received, where)
    r1 = lax.ppermute(r0, "exp", shift_y(1))
    r2 = lax.ppermute(r0, "exp", shift_y(-1))
    r3a = lax.ppermute(r1[:2], "exp", shift_y(1))
    r3b = lax.ppermute(r2[2:], "exp", shift_y(-1))
    rs = [r.reshape((r.shape[0], 2, 2) + r.shape[2:]) for r in (r0, r1, r2, r3a, r3b)]
    outs = attend(jnp.concatenate([where, usable]), qs, rs)
    back = [outs[0]] + [lax.ppermute(outs[d], "exp", shift_x(-d)) for d in range(1, SIDE)]
    return join_heads(back, where)


def ffn_kernel(x_ref, g0, u0, d0, g1, u1, d1, o_ref, acc):
    i = pl.program_id(0)
    half = pl.num_programs(0) // 2

    def run(g, u, d):
        gate = jnp.dot(x_ref[...], g[...], preferred_element_type=jnp.float32)
        up = jnp.dot(x_ref[...], u[...], preferred_element_type=jnp.float32)
        act = (gate / (1.0 + jnp.exp(-gate)) * up).astype(jnp.bfloat16)
        return jnp.dot(act, d[...], preferred_element_type=jnp.float32)

    @pl.when(i == 0)
    def _():
        acc[...] = run(g0, u0, d0)

    @pl.when((i > 0) & (i < half))
    def _():
        acc[...] += run(g0, u0, d0)

    @pl.when((i >= half) & (i < 2 * half - 1))
    def _():
        acc[...] += run(g1, u1, d1)

    @pl.when(i == 2 * half - 1)
    def _():
        o_ref[...] = (acc[...] + run(g1, u1, d1)).astype(jnp.bfloat16)


def expert_rows(rows, weights):
    tokens, width = rows.shape
    hidden = weights[0].shape[1]
    block = 128
    steps = hidden // block
    first = lambda i: jnp.minimum(i, steps - 1)
    second = lambda i: jnp.maximum(i - steps, 0)
    specs = []
    for at in (first, second):
        specs.append(pl.BlockSpec((width, block), lambda i, at=at: (0, at(i))))
        specs.append(pl.BlockSpec((width, block), lambda i, at=at: (0, at(i))))
        specs.append(pl.BlockSpec((block, width), lambda i, at=at: (at(i), 0)))
    return pl.pallas_call(
        ffn_kernel,
        grid=(2 * steps,),
        in_specs=[pl.BlockSpec((tokens, width), lambda i: (0, 0), pipeline_mode=pl.Buffered(1))] + specs,
        out_specs=pl.BlockSpec((tokens, width), lambda i: (0, 0), pipeline_mode=pl.Buffered(1)),
        out_shape=jax.ShapeDtypeStruct((tokens, width), jnp.bfloat16),
        scratch_shapes=[pltpu.VMEM((tokens, width), jnp.float32)],
        compiler_params=ordinary(56),
        cost_estimate=pl.CostEstimate(
            flops=12 * tokens * width * hidden,
            bytes_accessed=12 * width * hidden + 4 * tokens * width,
            transcendentals=2 * tokens * hidden,
        ),
        name="expert_rows",
    )(rows, *weights)


def route_experts(hidden, router, expert_ids, w_gate, w_up, w_down):
    expert_table = router.shape[1]
    local_tokens = hidden.shape[0]
    model_width = hidden.shape[1]
    capacity = max(2, 2 * local_tokens // expert_table)
    exp_count = lax.axis_size("exp")
    own = (w_gate[0], w_up[0], w_down[0])
    other = tuple(lax.ppermute(w, "ctx", CORE_SWAP) for w in own)
    logits = jnp.dot(hidden, router, preferred_element_type=jnp.float32)
    selected_expert = expert_ids[:, 0]
    onehot = (selected_expert[:, None] == jnp.arange(expert_table)[None, :]).astype(jnp.float32)
    gate_score = jax.nn.sigmoid(jnp.sum(logits * onehot, axis=1))
    scaled_scores = (hidden.astype(jnp.float32) * gate_score[:, None]).astype(jnp.bfloat16)
    slot_rank = (jnp.sum(jnp.cumsum(onehot, axis=0) * onehot, axis=1) - 1.0).astype(jnp.int32)
    dispatch = (
        (selected_expert[None, None, :] == jnp.arange(expert_table)[:, None, None])
        & (slot_rank[None, None, :] == jnp.arange(capacity)[None, :, None])
    ).astype(jnp.bfloat16)
    outgoing = jnp.einsum(
        "ect,td->ecd", dispatch, scaled_scores, preferred_element_type=jnp.float32
    ).astype(jnp.bfloat16)
    incoming = lax.all_to_all(outgoing, "exp", split_axis=0, concat_axis=0, tiled=True)
    rows = lax.all_gather(
        incoming.reshape(-1, model_width), "ctx", axis=0, tiled=True, axis_index_groups=RINGS
    )
    partial = expert_rows(rows, own + other)
    summed_output = lax.psum_scatter(
        partial, "ctx", scatter_dimension=0, tiled=True, axis_index_groups=RINGS
    )
    returned = lax.all_to_all(
        summed_output.reshape(exp_count, capacity, model_width),
        "exp",
        split_axis=0,
        concat_axis=0,
        tiled=True,
    )
    return jnp.einsum("ect,ecd->td", dispatch, returned, preferred_element_type=jnp.float32).astype(
        jnp.bfloat16
    )


def shards(
    queries,
    key_states,
    value_state_rows,
    block_lists,
    hidden,
    router,
    expert_ids,
    w_gate,
    w_up,
    w_down,
):
    attention = attend_all(queries, key_states, value_state_rows, block_lists)
    moe_out = route_experts(hidden, router, expert_ids, w_gate, w_up, w_down)
    return (attention, moe_out)


def solution(mesh):
    placed = (
        P(None, ("ctx", "exp"), None),
        P(None, ("ctx", "exp"), None),
        P(None, ("ctx", "exp"), None),
        P(),
        P(("ctx", "exp"), None),
        P(),
        P(("ctx", "exp"), None),
        P("exp", None, "ctx"),
        P("exp", None, "ctx"),
        P("exp", "ctx", None),
    )
    return jax.shard_map(
        shards,
        mesh=mesh,
        in_specs=placed,
        out_specs=(P(None, ("ctx", "exp"), None), P(("ctx", "exp"), None)),
        check_vma=False,
    )
```

```python
import functools

import jax
import jax.numpy as jnp
from jax import lax
from jax.experimental import pallas as pl
from jax.experimental.pallas import tpu as pltpu
from jax.sharding import PartitionSpec as P

HEAD_DIM = 128
NEGATIVE_LARGE = -1e30
SIDE = 4
RINGS = [[2 * z + c for z in range(8)] for c in range(2)]
CORE_SWAP = [(i, i ^ 1) for i in range(16)]


def shift_x(d):
    return [(4 * a + b, 4 * ((a + d) % 4) + b) for a in range(4) for b in range(4)]


def shift_y(d):
    return [(4 * a + b, 4 * a + (b + d) % 4) for a in range(4) for b in range(4)]


def ordinary(vmem=48):
    return pltpu.CompilerParams(
        dimension_semantics=("arbitrary",), vmem_limit_bytes=vmem * 1024 * 1024
    )


def pick_kernel(table, source, *outs):
    x = table[4]
    for d in range(SIDE):
        h = lax.rem(x + d, SIDE)
        outs[d][0] = source[0, :, pl.ds(pl.multiple_of(h * 256, 256), 256)]


def pick_heads(everyone, table):
    rows, width = everyone.shape[1], everyone.shape[2]
    part = jax.ShapeDtypeStruct((4, rows, 256), everyone.dtype)
    return pl.pallas_call(
        pick_kernel,
        grid_spec=pltpu.PrefetchScalarGridSpec(
            num_scalar_prefetch=1,
            grid=(4,),
            in_specs=[pl.BlockSpec((1, rows, width), lambda i, t: (t[i], 0, 0))],
            out_specs=[pl.BlockSpec((1, rows, 256), lambda i, t: (i, 0, 0))] * SIDE,
        ),
        out_shape=[part] * SIDE,
        compiler_params=ordinary(16),
        cost_estimate=pl.CostEstimate(flops=0, bytes_accessed=2 << 20, transcendentals=0),
        name="pick_heads",
    )(table, everyone)


def split_kernel(where, source, *outs):
    x = where[0]
    width = outs[0].shape[2]
    for d in range(SIDE):
        h = lax.rem(x + d, SIDE)
        outs[d][...] = source[:, :, pl.ds(pl.multiple_of(h * width, 128), width)]


def split_queries(queries, where):
    part = jax.ShapeDtypeStruct(queries.shape[:2] + (queries.shape[2] // SIDE,), queries.dtype)
    return pl.pallas_call(
        split_kernel,
        grid_spec=pltpu.PrefetchScalarGridSpec(
            num_scalar_prefetch=1,
            grid=(1,),
            in_specs=[pl.BlockSpec(queries.shape, lambda i, t: (0, 0, 0))],
            out_specs=[pl.BlockSpec(part.shape, lambda i, t: (0, 0, 0))] * SIDE,
        ),
        out_shape=[part] * SIDE,
        compiler_params=ordinary(16),
        cost_estimate=pl.CostEstimate(flops=0, bytes_accessed=1310720, transcendentals=0),
        name="split_queries",
    )(where, queries)


def stack_kernel(where, *refs):
    x = where[0]
    out = refs[SIDE]
    for d in range(SIDE):
        out[lax.rem(x + SIDE - d, SIDE)] = refs[d][...]


def stack_sources(parts, where):
    shape = parts[0].shape
    zeros = (0,) * len(shape)
    return pl.pallas_call(
        stack_kernel,
        grid_spec=pltpu.PrefetchScalarGridSpec(
            num_scalar_prefetch=1,
            grid=(1,),
            in_specs=[pl.BlockSpec(shape, lambda i, t: zeros)] * SIDE,
            out_specs=pl.BlockSpec((SIDE,) + shape, lambda i, t: (0,) + zeros),
        ),
        out_shape=jax.ShapeDtypeStruct((SIDE,) + shape, parts[0].dtype),
        compiler_params=ordinary(16),
        cost_estimate=pl.CostEstimate(flops=0, bytes_accessed=1 << 20, transcendentals=0),
        name="stack_sources",
    )(where, *parts)


def join_kernel(where, *refs):
    x = where[0]
    out = refs[SIDE]
    width = refs[0].shape[2]
    for d in range(SIDE):
        h = lax.rem(x + d, SIDE)
        out[:, :, pl.ds(pl.multiple_of(h * width, 128), width)] = refs[d][...]


def join_heads(parts, where):
    shape = parts[0].shape
    full = shape[:2] + (shape[2] * SIDE,)
    return pl.pallas_call(
        join_kernel,
        grid_spec=pltpu.PrefetchScalarGridSpec(
            num_scalar_prefetch=1,
            grid=(1,),
            in_specs=[pl.BlockSpec(shape, lambda i, t: (0, 0, 0))] * SIDE,
            out_specs=pl.BlockSpec(full, lambda i, t: (0, 0, 0)),
        ),
        out_shape=jax.ShapeDtypeStruct(full, parts[0].dtype),
        compiler_params=ordinary(16),
        cost_estimate=pl.CostEstimate(flops=0, bytes_accessed=1310720, transcendentals=0),
        name="join_heads",
    )(where, *parts)


NT = (((1,), (1,)), ((), ()))


def attend_kernel(where, q0, q1, q2, q3, r0, r1, r2, r3a, r3b, o0, o1, o2, o3, kown, vown, klist, vlist, qall, oall):
    p = pl.program_id(0)
    x, y, usable = where[0], where[1], where[2 + p]
    pieces = (r0, r1, r2)
    for xs in range(SIDE):
        last = r3a if xs < 2 else r3b
        for turn in range(SIDE):
            piece = pieces[turn][xs] if turn < 3 else last[xs % 2]
            at = pl.ds(xs * 256 + turn * 64, 64)
            kown[at, :] = piece[0, 0, :, :HEAD_DIM]
            vown[at, :] = piece[0, 0, :, HEAD_DIM:]
            klist[at, :] = piece[1, 0, :, :HEAD_DIM]
            vlist[at, :] = piece[1, 0, :, HEAD_DIM:]
    scaling = HEAD_DIM ** (-0.5)
    group = q0.shape[2] // HEAD_DIM
    rows = 64 * group
    qs, outs = (q0, q1, q2, q3), (o0, o1, o2, o3)
    query_row = lax.rem(lax.broadcasted_iota(jnp.int32, (rows, 256), 0), 64)
    key_index = lax.broadcasted_iota(jnp.int32, (rows, 256), 1)
    turn = key_index // 64
    behind = jnp.where(turn == 0, 0, jnp.where(turn == 1, 3, jnp.where(turn == 2, 1, 2)))
    key_pos = lax.rem(y + behind, SIDE) * 64 + lax.rem(key_index, 64)
    diagonal = key_pos <= y * 64 + query_row
    for d in range(SIDE):
        qall[lax.rem(x + SIDE - d, SIDE)] = qs[d][0]
    for case in range(SIDE):
        query = jnp.concatenate(
            [qall[case, :, g * HEAD_DIM : (g + 1) * HEAD_DIM] for g in range(group)], axis=0
        )
        before = case * 256
        own = lax.dot_general(
            query, kown[pl.ds(before, 256), :], NT, preferred_element_type=jnp.float32
        )
        own = jnp.where(diagonal, own * scaling, NEGATIVE_LARGE)
        far = lax.dot_general(query, klist[...], NT, preferred_element_type=jnp.float32)
        far = jnp.where(usable > 0, far * scaling, NEGATIVE_LARGE)
        top = jnp.maximum(jnp.max(own, axis=1, keepdims=True), jnp.max(far, axis=1, keepdims=True))
        if case:
            near = lax.dot_general(
                query, kown[pl.ds(0, before), :], NT, preferred_element_type=jnp.float32
            )
            near = near * scaling
            top = jnp.maximum(top, jnp.max(near, axis=1, keepdims=True))
        own = jnp.exp(own - top)
        far = jnp.exp(far - top)
        total = jnp.sum(own, axis=1, keepdims=True) + jnp.sum(far, axis=1, keepdims=True)
        mixed = jnp.dot(
            own.astype(jnp.bfloat16), vown[pl.ds(before, 256), :], preferred_element_type=jnp.float32
        ) + jnp.dot(far.astype(jnp.bfloat16), vlist[...], preferred_element_type=jnp.float32)
        if case:
            near = jnp.exp(near - top)
            total = total + jnp.sum(near, axis=1, keepdims=True)
            mixed = mixed + jnp.dot(
                near.astype(jnp.bfloat16),
                vown[pl.ds(0, before), :],
                preferred_element_type=jnp.float32,
            )
        mixed = (mixed / total).astype(jnp.bfloat16)
        for g in range(group):
            oall[case, :, g * HEAD_DIM : (g + 1) * HEAD_DIM] = mixed[g * 64 : (g + 1) * 64]
    for d in range(SIDE):
        outs[d][0] = oall[lax.rem(x + SIDE - d, SIDE)]


def attend(where, qs, rs):
    qspec = pl.BlockSpec((1,) + qs[0].shape[1:], lambda i, t: (i, 0, 0))

    def rspec(r):
        return pl.BlockSpec((r.shape[0], 2, 1) + r.shape[3:], lambda i, t: (0, 0, i, 0, 0))

    return pl.pallas_call(
        attend_kernel,
        grid_spec=pltpu.PrefetchScalarGridSpec(
            num_scalar_prefetch=1,
            grid=(2,),
            in_specs=[qspec] * SIDE + [rspec(r) for r in rs],
            out_specs=[qspec] * SIDE,
            scratch_shapes=[pltpu.VMEM((1024, HEAD_DIM), jnp.bfloat16)] * 4
            + [pltpu.VMEM((SIDE,) + qs[0].shape[1:], jnp.bfloat16)] * 2,
        ),
        out_shape=[jax.ShapeDtypeStruct(q.shape, q.dtype) for q in qs],
        compiler_params=ordinary(40),
        cost_estimate=pl.CostEstimate(
            flops=2200000000, bytes_accessed=4 << 20, transcendentals=4300000
        ),
        name="attend",
    )(where, *qs, *rs)


def pair_rows(key_states, value_state_rows):
    heads = key_states.shape[2] // HEAD_DIM
    columns = []
    for h in range(heads):
        columns.append(key_states[:, :, h * HEAD_DIM : (h + 1) * HEAD_DIM])
        columns.append(value_state_rows[:, :, h * HEAD_DIM : (h + 1) * HEAD_DIM])
    return jnp.concatenate(columns, axis=2)


def attend_all(queries, everyone, block_lists):
    ctx_count = lax.axis_size("ctx")
    blocks_total = 2 * ctx_count
    ctx_index = lax.axis_index("ctx")
    exp_index = lax.axis_index("exp")
    x, y = lax.div(exp_index, SIDE), lax.rem(exp_index, SIDE)
    where = jnp.stack([x, y]).astype(jnp.int32)
    own_blocks = jnp.stack([ctx_index, blocks_total - 1 - ctx_index])
    listed = block_lists[own_blocks]
    usable = (listed != own_blocks).astype(jnp.int32)
    wanted = jnp.concatenate([own_blocks, listed])
    holder = jnp.minimum(wanted, blocks_total - 1 - wanted)
    row = 2 * holder + (wanted >= ctx_count).astype(jnp.int32)
    table = jnp.concatenate([row, x[None]]).astype(jnp.int32)

    mine = split_queries(queries, where)
    qs = [mine[0]] + [lax.ppermute(mine[d], "exp", shift_x(d)) for d in range(1, SIDE)]
    picked = pick_heads(everyone, table)
    received = [picked[0]] + [lax.ppermute(picked[d], "exp", shift_x(d)) for d in range(1, SIDE)]
    r0 = stack_sources(received, where)
    r1 = lax.ppermute(r0, "exp", shift_y(1))
    r2 = lax.ppermute(r0, "exp", shift_y(-1))
    r3a = lax.ppermute(r1[:2], "exp", shift_y(1))
    r3b = lax.ppermute(r2[2:], "exp", shift_y(-1))
    rs = [r.reshape((r.shape[0], 2, 2) + r.shape[2:]) for r in (r0, r1, r2, r3a, r3b)]
    outs = attend(jnp.concatenate([where, usable]), qs, rs)
    back = [outs[0]] + [lax.ppermute(outs[d], "exp", shift_x(-d)) for d in range(1, SIDE)]
    return join_heads(back, where)


def ffn_kernel(counts, width, hidden, *refs):
    n, m = counts
    xs, ws, outs = refs[:n], refs[n : n + 6], refs[n + 6 : n + 6 + m]
    x_all, gates, downs, sums, sems = refs[n + 6 + m :]
    targets = [gates.at[0], gates.at[1], gates.at[2], gates.at[3]]
    targets += [downs.at[pl.ds(0, hidden), :], downs.at[pl.ds(hidden, hidden), :]]
    order = (0, 1, 3, 4, 2, 5)
    copies = [pltpu.make_async_copy(ws[w], targets[k], sems.at[k]) for k, w in enumerate(order)]
    for copy in copies:
        copy.start()
    at = 0
    for x in xs:
        x_all[pl.ds(at, x.shape[0]), :] = x[...]
        at += x.shape[0]
    acts = []
    depth = 1024

    def project(which):
        sums[...] = jnp.zeros_like(sums)

        @pl.loop(0, width // depth)
        def _(k):
            span = pl.ds(pl.multiple_of(k * depth, depth), depth)
            sums[...] += jnp.dot(
                x_all[:, span], gates[which, span, :], preferred_element_type=jnp.float32
            )

        return sums[...]

    for half in range(2):
        copies[2 * half].wait()
        gate = project(2 * half)
        gate = gate / (1.0 + jnp.exp(-gate))
        copies[2 * half + 1].wait()
        acts.append((gate * project(2 * half + 1)).astype(jnp.bfloat16))
    act = jnp.concatenate(acts, axis=1)
    copies[4].wait()
    copies[5].wait()
    block = 512

    @pl.loop(0, width // block)
    def _(k):
        columns = pl.ds(pl.multiple_of(k * block, block), block)
        part = jnp.dot(act, downs[:, columns], preferred_element_type=jnp.float32)
        part = part.astype(jnp.bfloat16)
        at = 0
        for out in outs:
            out[:, columns] = part[at : at + out.shape[0]]
            at += out.shape[0]


def expert_rows(xs, weights, out_rows):
    width = xs[0].shape[1]
    hidden = weights[0].shape[1]
    tokens = sum(x.shape[0] for x in xs)
    whole = pl.BlockSpec(memory_space=pltpu.VMEM)
    return pl.pallas_call(
        functools.partial(ffn_kernel, (len(xs), len(out_rows)), width, hidden),
        in_specs=[whole] * len(xs) + [pl.BlockSpec(memory_space=pl.ANY)] * 6,
        out_specs=[whole] * len(out_rows),
        out_shape=[jax.ShapeDtypeStruct((r, width), jnp.bfloat16) for r in out_rows],
        scratch_shapes=[
            pltpu.VMEM((tokens, width), jnp.bfloat16),
            pltpu.VMEM((4, width, hidden), jnp.bfloat16),
            pltpu.VMEM((2 * hidden, width), jnp.bfloat16),
            pltpu.VMEM((tokens, hidden), jnp.float32),
            pltpu.SemaphoreType.DMA((6,)),
        ],
        compiler_params=pltpu.CompilerParams(vmem_limit_bytes=40 * 1024 * 1024),
        cost_estimate=pl.CostEstimate(
            flops=12 * tokens * width * hidden,
            bytes_accessed=12 * width * hidden + 4 * tokens * width,
            transcendentals=2 * tokens * hidden,
        ),
        name="expert_rows",
    )(*xs, *weights)


def ring(d):
    return [(2 * z + c, 2 * ((z + d) % 8) + c) for z in range(8) for c in range(2)]


def up_z(v):
    return lax.ppermute(v, "ctx", ring(1))


def down_z(v):
    return lax.ppermute(v, "ctx", ring(-1))


def add(a, b):
    return (a.astype(jnp.float32) + b.astype(jnp.float32)).astype(jnp.bfloat16)


def ring_experts(block, first, gathered, weights):
    rows = block.shape[0]
    half = rows // 2
    below, above = [block, first[0]], [block, first[1]]
    for k in range(2):
        below.append(up_z(below[-1]))
        above.append(down_z(above[-1]))
    far_low, far_high = up_z(below[3][:half]), down_z(above[3][half:])
    near = expert_rows(
        [block, below[1], above[1], below[2], above[2]], weights, [rows] * 5
    )
    near, far_low, far_high = lax.optimization_barrier((near, far_low, far_high))
    own, p_b1, p_a1, p_b2, p_a2 = near
    p_low, p_high, p_b3, p_a3, p_gathered = expert_rows(
        [far_low, far_high, below[3], above[3], gathered],
        weights,
        [half, half, rows, rows, gathered.shape[0]],
    )
    rise, fall = up_z(p_low), down_z(p_high)
    rise = jnp.concatenate([add(rise, p_a3[:half]), p_a3[half:]], axis=0)
    fall = jnp.concatenate([p_b3[:half], add(fall, p_b3[half:])], axis=0)
    rise, fall = up_z(rise), down_z(fall)
    rise, fall = up_z(add(rise, p_a2)), down_z(add(fall, p_b2))
    rise, fall = up_z(add(rise, p_a1)), down_z(add(fall, p_b1))
    total = rise.astype(jnp.float32) + fall.astype(jnp.float32) + own.astype(jnp.float32)
    return total.astype(jnp.bfloat16), p_gathered


def route_experts(hidden, router, expert_ids, w_gate, w_up, w_down, everyone):
    expert_table = router.shape[1]
    local_tokens = hidden.shape[0]
    model_width = hidden.shape[1]
    capacity = max(2, 2 * local_tokens // expert_table)
    exp_count = lax.axis_size("exp")
    own = (w_gate[0], w_up[0], w_down[0])
    other = tuple(lax.ppermute(w, "ctx", CORE_SWAP) for w in own)
    weights = own + other
    logits = jnp.dot(hidden, router, preferred_element_type=jnp.float32)
    selected_expert = expert_ids[:, 0]
    onehot = (selected_expert[:, None] == jnp.arange(expert_table)[None, :]).astype(jnp.float32)
    gate_score = jax.nn.sigmoid(jnp.sum(logits * onehot, axis=1))
    scaled_scores = (hidden.astype(jnp.float32) * gate_score[:, None]).astype(jnp.bfloat16)
    slot_rank = (jnp.sum(jnp.cumsum(onehot, axis=0) * onehot, axis=1) - 1.0).astype(jnp.int32)
    dispatch = (
        (selected_expert[None, None, :] == jnp.arange(expert_table)[:, None, None])
        & (slot_rank[None, None, :] == jnp.arange(capacity)[None, :, None])
    ).astype(jnp.bfloat16)
    outgoing = jnp.einsum(
        "ect,td->ecd", dispatch, scaled_scores, preferred_element_type=jnp.float32
    ).astype(jnp.bfloat16)
    incoming = lax.all_to_all(outgoing, "exp", split_axis=0, concat_axis=0, tiled=True)
    incoming = incoming.reshape(-1, model_width)
    split = incoming.shape[0] * 3 // 4
    kept = incoming[:split]
    first = (up_z(kept), down_z(kept))
    gathered_part, first, everyone = lax.optimization_barrier((incoming[split:], first, everyone))
    rows = lax.all_gather(gathered_part, "ctx", axis=0, tiled=True, axis_index_groups=RINGS)
    ringed, partial = ring_experts(kept, first, rows, weights)
    scattered = lax.psum_scatter(
        partial, "ctx", scatter_dimension=0, tiled=True, axis_index_groups=RINGS
    )
    summed_output = jnp.concatenate([ringed, scattered], axis=0)
    returned = lax.all_to_all(
        summed_output.reshape(exp_count, capacity, model_width),
        "exp",
        split_axis=0,
        concat_axis=0,
        tiled=True,
    )
    moe_out = jnp.einsum(
        "ect,ecd->td", dispatch, returned, preferred_element_type=jnp.float32
    ).astype(jnp.bfloat16)
    return moe_out, everyone


def shards(
    queries,
    key_states,
    value_state_rows,
    block_lists,
    hidden,
    router,
    expert_ids,
    w_gate,
    w_up,
    w_down,
):
    paired = pair_rows(key_states, value_state_rows)
    everyone = lax.all_gather(paired, "ctx", axis=0, tiled=True)
    moe_out, everyone = route_experts(
        hidden, router, expert_ids, w_gate, w_up, w_down, everyone
    )
    attention = attend_all(queries, everyone, block_lists)
    return (attention, moe_out)


def solution(mesh):
    placed = (
        P(None, ("ctx", "exp"), None),
        P(None, ("ctx", "exp"), None),
        P(None, ("ctx", "exp"), None),
        P(),
        P(("ctx", "exp"), None),
        P(),
        P(("ctx", "exp"), None),
        P("exp", None, "ctx"),
        P("exp", None, "ctx"),
        P("exp", "ctx", None),
    )
    return jax.shard_map(
        shards,
        mesh=mesh,
        in_specs=placed,
        out_specs=(P(None, ("ctx", "exp"), None), P(("ctx", "exp"), None)),
        check_vma=False,
    )
```

```python
import functools

import jax
import jax.numpy as jnp
from jax import lax
from jax.experimental import pallas as pl
from jax.experimental.pallas import tpu as pltpu
from jax.sharding import PartitionSpec as P

HEAD_DIM = 128
NEGATIVE_LARGE = -1e30
SIDE = 4
RINGS = [[2 * z + c for z in range(8)] for c in range(2)]
CORE_SWAP = [(i, i ^ 1) for i in range(16)]


def shift_x(d):
    return [(4 * a + b, 4 * ((a + d) % 4) + b) for a in range(4) for b in range(4)]


def shift_y(d):
    return [(4 * a + b, 4 * a + (b + d) % 4) for a in range(4) for b in range(4)]


def ordinary(vmem=48):
    return pltpu.CompilerParams(
        dimension_semantics=("arbitrary",), vmem_limit_bytes=vmem * 1024 * 1024
    )


WHOLE = pl.BlockSpec(memory_space=pltpu.VMEM)
TABLE = pl.BlockSpec(memory_space=pltpu.SMEM)


def small(kernel, outs, name, moved, scratch=()):
    return functools.partial(
        pl.pallas_call,
        kernel,
        out_shape=outs,
        scratch_shapes=scratch,
        compiler_params=pltpu.CompilerParams(vmem_limit_bytes=16 * 1024 * 1024),
        cost_estimate=pl.CostEstimate(flops=0, bytes_accessed=moved, transcendentals=0),
        name=name,
    )


def pair_kernel(keys, values, out):
    for h in range(SIDE):
        out[:, :, h * 256 : h * 256 + 128] = keys[:, :, h * 128 : h * 128 + 128]
        out[:, :, h * 256 + 128 : h * 256 + 256] = values[:, :, h * 128 : h * 128 + 128]


def pair_rows(keys, values):
    shape = keys.shape[:2] + (2 * keys.shape[2],)
    call = small(pair_kernel, jax.ShapeDtypeStruct(shape, keys.dtype), "pair_rows", 1 << 19)
    return call(in_specs=[WHOLE] * 2, out_specs=WHOLE)(keys, values)


def ring(d):
    return [(2 * z + c, 2 * ((z + d) % 8) + c) for z in range(8) for c in range(2)]


def up_z(v):
    return lax.ppermute(v, "ctx", ring(1))


def down_z(v):
    return lax.ppermute(v, "ctx", ring(-1))


def choose_kernel(table, *refs):
    own, b1, b2, b3, far_low, far_high, a3, a2, a1, mine, theirs, held = refs
    for k, block in ((0, own), (1, b1), (2, b2), (3, b3), (5, a3), (6, a2), (7, a1)):
        held[2 * k] = block[0]
        held[2 * k + 1] = block[1]
    held[8] = far_low[0]
    held[9] = far_high[0]
    for i in range(2):
        mine[i] = held[table[i]]
        theirs[i] = held[table[2 + i]]


def choose_blocks(paired, table):
    below, above = [paired], [paired]
    for _ in range(3):
        below.append(up_z(below[-1]))
        above.append(down_z(above[-1]))
    far_low, far_high = up_z(below[3][:1]), down_z(above[3][1:])
    out = jax.ShapeDtypeStruct(paired.shape, paired.dtype)
    held = pltpu.VMEM((16,) + paired.shape[1:], paired.dtype)
    call = small(choose_kernel, [out, out], "choose_blocks", 3 << 20, [held])
    return call(in_specs=[TABLE] + [WHOLE] * 9, out_specs=[WHOLE] * 2)(
        table, paired, *below[1:], far_low, far_high, above[3], above[2], above[1]
    )


def pick_kernel(table, own, mine, swapped, *outs):
    x = table[0]
    for d in range(SIDE):
        h = lax.rem(x + d, SIDE)
        columns = pl.ds(pl.multiple_of(h * 256, 256), 256)
        outs[d][0:2] = own[:, :, columns]
        for i in range(2):
            here = table[1 + i] > 0
            outs[d][2 + i] = jnp.where(here, mine[i, :, columns], swapped[i, :, columns])


def pick_heads(own, mine, swapped, table):
    rows = own.shape[1]
    part = jax.ShapeDtypeStruct((4, rows, 256), own.dtype)
    call = small(pick_kernel, [part] * SIDE, "pick_heads", 2 << 20)
    return call(in_specs=[TABLE] + [WHOLE] * 3, out_specs=[WHOLE] * SIDE)(
        table, own, mine, swapped
    )


def split_kernel(where, source, *outs):
    x = where[0]
    width = outs[0].shape[2]
    for d in range(SIDE):
        h = lax.rem(x + d, SIDE)
        outs[d][...] = source[:, :, pl.ds(pl.multiple_of(h * width, 128), width)]


def split_queries(queries, where):
    part = jax.ShapeDtypeStruct(queries.shape[:2] + (queries.shape[2] // SIDE,), queries.dtype)
    return pl.pallas_call(
        split_kernel,
        grid_spec=pltpu.PrefetchScalarGridSpec(
            num_scalar_prefetch=1,
            grid=(1,),
            in_specs=[pl.BlockSpec(queries.shape, lambda i, t: (0, 0, 0))],
            out_specs=[pl.BlockSpec(part.shape, lambda i, t: (0, 0, 0))] * SIDE,
        ),
        out_shape=[part] * SIDE,
        compiler_params=ordinary(16),
        cost_estimate=pl.CostEstimate(flops=0, bytes_accessed=1310720, transcendentals=0),
        name="split_queries",
    )(where, queries)


def stack_kernel(where, *refs):
    x = where[0]
    out = refs[SIDE]
    for d in range(SIDE):
        out[lax.rem(x + SIDE - d, SIDE)] = refs[d][...]


def stack_sources(parts, where):
    shape = parts[0].shape
    zeros = (0,) * len(shape)
    return pl.pallas_call(
        stack_kernel,
        grid_spec=pltpu.PrefetchScalarGridSpec(
            num_scalar_prefetch=1,
            grid=(1,),
            in_specs=[pl.BlockSpec(shape, lambda i, t: zeros)] * SIDE,
            out_specs=pl.BlockSpec((SIDE,) + shape, lambda i, t: (0,) + zeros),
        ),
        out_shape=jax.ShapeDtypeStruct((SIDE,) + shape, parts[0].dtype),
        compiler_params=ordinary(16),
        cost_estimate=pl.CostEstimate(flops=0, bytes_accessed=1 << 20, transcendentals=0),
        name="stack_sources",
    )(where, *parts)


def join_kernel(where, *refs):
    x = where[0]
    out = refs[SIDE]
    width = refs[0].shape[2]
    for d in range(SIDE):
        h = lax.rem(x + d, SIDE)
        out[:, :, pl.ds(pl.multiple_of(h * width, 128), width)] = refs[d][...]


def join_heads(parts, where):
    shape = parts[0].shape
    full = shape[:2] + (shape[2] * SIDE,)
    return pl.pallas_call(
        join_kernel,
        grid_spec=pltpu.PrefetchScalarGridSpec(
            num_scalar_prefetch=1,
            grid=(1,),
            in_specs=[pl.BlockSpec(shape, lambda i, t: (0, 0, 0))] * SIDE,
            out_specs=pl.BlockSpec(full, lambda i, t: (0, 0, 0)),
        ),
        out_shape=jax.ShapeDtypeStruct(full, parts[0].dtype),
        compiler_params=ordinary(16),
        cost_estimate=pl.CostEstimate(flops=0, bytes_accessed=1310720, transcendentals=0),
        name="join_heads",
    )(where, *parts)


NT = (((1,), (1,)), ((), ()))


def attend_kernel(where, q0, q1, q2, q3, r0, r1, r2, r3a, r3b, o0, o1, o2, o3, kown, vown, klist, vlist, qall, oall):
    p = pl.program_id(0)
    x, y, usable = where[0], where[1], where[2 + p]
    pieces = (r0, r1, r2)
    for xs in range(SIDE):
        last = r3a if xs < 2 else r3b
        for turn in range(SIDE):
            piece = pieces[turn][xs] if turn < 3 else last[xs % 2]
            at = pl.ds(xs * 256 + turn * 64, 64)
            kown[at, :] = piece[0, 0, :, :HEAD_DIM]
            vown[at, :] = piece[0, 0, :, HEAD_DIM:]
            klist[at, :] = piece[1, 0, :, :HEAD_DIM]
            vlist[at, :] = piece[1, 0, :, HEAD_DIM:]
    scaling = HEAD_DIM ** (-0.5)
    group = q0.shape[2] // HEAD_DIM
    rows = 64 * group
    qs, outs = (q0, q1, q2, q3), (o0, o1, o2, o3)
    query_row = lax.rem(lax.broadcasted_iota(jnp.int32, (rows, 256), 0), 64)
    key_index = lax.broadcasted_iota(jnp.int32, (rows, 256), 1)
    turn = key_index // 64
    behind = jnp.where(turn == 0, 0, jnp.where(turn == 1, 3, jnp.where(turn == 2, 1, 2)))
    key_pos = lax.rem(y + behind, SIDE) * 64 + lax.rem(key_index, 64)
    diagonal = key_pos <= y * 64 + query_row
    for d in range(SIDE):
        qall[lax.rem(x + SIDE - d, SIDE)] = qs[d][0]
    for case in range(SIDE):
        query = jnp.concatenate(
            [qall[case, :, g * HEAD_DIM : (g + 1) * HEAD_DIM] for g in range(group)], axis=0
        )
        before = case * 256
        own = lax.dot_general(
            query, kown[pl.ds(before, 256), :], NT, preferred_element_type=jnp.float32
        )
        own = jnp.where(diagonal, own * scaling, NEGATIVE_LARGE)
        far = lax.dot_general(query, klist[...], NT, preferred_element_type=jnp.float32)
        far = jnp.where(usable > 0, far * scaling, NEGATIVE_LARGE)
        top = jnp.maximum(jnp.max(own, axis=1, keepdims=True), jnp.max(far, axis=1, keepdims=True))
        if case:
            near = lax.dot_general(
                query, kown[pl.ds(0, before), :], NT, preferred_element_type=jnp.float32
            )
            near = near * scaling
            top = jnp.maximum(top, jnp.max(near, axis=1, keepdims=True))
        own = jnp.exp(own - top)
        far = jnp.exp(far - top)
        total = jnp.sum(own, axis=1, keepdims=True) + jnp.sum(far, axis=1, keepdims=True)
        mixed = jnp.dot(
            own.astype(jnp.bfloat16), vown[pl.ds(before, 256), :], preferred_element_type=jnp.float32
        ) + jnp.dot(far.astype(jnp.bfloat16), vlist[...], preferred_element_type=jnp.float32)
        if case:
            near = jnp.exp(near - top)
            total = total + jnp.sum(near, axis=1, keepdims=True)
            mixed = mixed + jnp.dot(
                near.astype(jnp.bfloat16),
                vown[pl.ds(0, before), :],
                preferred_element_type=jnp.float32,
            )
        mixed = (mixed / total).astype(jnp.bfloat16)
        for g in range(group):
            oall[case, :, g * HEAD_DIM : (g + 1) * HEAD_DIM] = mixed[g * 64 : (g + 1) * 64]
    for d in range(SIDE):
        outs[d][0] = oall[lax.rem(x + SIDE - d, SIDE)]


def attend(where, qs, rs):
    qspec = pl.BlockSpec((1,) + qs[0].shape[1:], lambda i, t: (i, 0, 0))

    def rspec(r):
        return pl.BlockSpec((r.shape[0], 2, 1) + r.shape[3:], lambda i, t: (0, 0, i, 0, 0))

    return pl.pallas_call(
        attend_kernel,
        grid_spec=pltpu.PrefetchScalarGridSpec(
            num_scalar_prefetch=1,
            grid=(2,),
            in_specs=[qspec] * SIDE + [rspec(r) for r in rs],
            out_specs=[qspec] * SIDE,
            scratch_shapes=[pltpu.VMEM((1024, HEAD_DIM), jnp.bfloat16)] * 4
            + [pltpu.VMEM((SIDE,) + qs[0].shape[1:], jnp.bfloat16)] * 2,
        ),
        out_shape=[jax.ShapeDtypeStruct(q.shape, q.dtype) for q in qs],
        compiler_params=ordinary(40),
        cost_estimate=pl.CostEstimate(
            flops=2200000000, bytes_accessed=4 << 20, transcendentals=4300000
        ),
        name="attend",
    )(where, *qs, *rs)


def exchange_rows(queries, key_states, value_state_rows, block_lists):
    ctx_count = lax.axis_size("ctx")
    blocks_total = 2 * ctx_count
    ctx_index = lax.axis_index("ctx")
    exp_index = lax.axis_index("exp")
    x, y = lax.div(exp_index, SIDE), lax.rem(exp_index, SIDE)
    z, core = lax.div(ctx_index, 2), lax.rem(ctx_index, 2)
    where = jnp.stack([x, y]).astype(jnp.int32)
    other = ctx_index + 1 - 2 * core
    own_blocks = jnp.stack(
        [ctx_index, blocks_total - 1 - ctx_index, other, blocks_total - 1 - other]
    )
    listed = block_lists[own_blocks]
    usable = (listed != own_blocks).astype(jnp.int32)
    holder = jnp.minimum(listed, blocks_total - 1 - listed)
    distance = lax.rem(z + 8 - lax.div(holder, 2), 8)
    chosen = (2 * distance + (listed >= ctx_count).astype(jnp.int32)).astype(jnp.int32)
    local = (lax.rem(holder, 2) == core).astype(jnp.int32)

    paired = pair_rows(key_states, value_state_rows)
    mine, theirs = choose_blocks(paired, chosen)
    swapped = lax.ppermute(theirs, "ctx", CORE_SWAP)
    picked = pick_heads(
        paired, mine, swapped, jnp.concatenate([x[None], local[:2]]).astype(jnp.int32)
    )
    split = split_queries(queries, where)
    qs = [split[0]] + [lax.ppermute(split[d], "exp", shift_x(d)) for d in range(1, SIDE)]
    received = [picked[0]] + [lax.ppermute(picked[d], "exp", shift_x(d)) for d in range(1, SIDE)]
    r0 = stack_sources(received, where)
    r1 = lax.ppermute(r0, "exp", shift_y(1))
    r2 = lax.ppermute(r0, "exp", shift_y(-1))
    r3a = lax.ppermute(r1[:2], "exp", shift_y(1))
    r3b = lax.ppermute(r2[2:], "exp", shift_y(-1))
    rs = [r.reshape((r.shape[0], 2, 2) + r.shape[2:]) for r in (r0, r1, r2, r3a, r3b)]
    return where, jnp.concatenate([where, usable[:2]]), qs, rs


def attend_all(where, state, qs, rs):
    outs = attend(state, qs, rs)
    back = [outs[0]] + [lax.ppermute(outs[d], "exp", shift_x(-d)) for d in range(1, SIDE)]
    return join_heads(back, where)


def ffn_kernel(counts, refs):
    xs, ws, outs = refs[:counts], refs[counts : counts + 6], refs[counts + 6 : 2 * counts + 6]
    rows, gates, downs, results, act, w_sem, x_sem, o_sem = refs[2 * counts + 6 :]
    width, hidden = gates.shape[1], gates.shape[2]
    step = rows.shape[1]
    parts = []
    for x, out in zip(xs, outs):
        for at in range(0, x.shape[0], step):
            parts.append((x, out, at, min(step, x.shape[0] - at)))
    loads = [
        pltpu.make_async_copy(
            x.at[pl.ds(at, n), :], rows.at[k, pl.ds(0, n), :], x_sem.at[k]
        )
        for k, (x, _, at, n) in enumerate(parts)
    ]
    stores = [
        pltpu.make_async_copy(
            results.at[k, pl.ds(0, n), :], out.at[pl.ds(at, n), :], o_sem.at[k]
        )
        for k, (_, out, at, n) in enumerate(parts)
    ]
    targets = [gates.at[0], gates.at[1], gates.at[2], gates.at[3]]
    targets += [downs.at[pl.ds(0, hidden), :], downs.at[pl.ds(hidden, hidden), :]]
    order = (0, 1, 3, 4, 2, 5)
    weights = [pltpu.make_async_copy(ws[w], targets[k], w_sem.at[k]) for k, w in enumerate(order)]
    loads[0].start()
    for copy in weights:
        copy.start()
    for copy in loads[1:]:
        copy.start()
    block = 1024
    for k, (x, out, at, n) in enumerate(parts):
        loads[k].wait()
        for half in range(2):
            if k == 0:
                weights[2 * half].wait()
            gate = jnp.dot(rows[k, :n], gates[2 * half], preferred_element_type=jnp.float32)
            if k == 0:
                weights[2 * half + 1].wait()
            up = jnp.dot(rows[k, :n], gates[2 * half + 1], preferred_element_type=jnp.float32)
            act[:n, half * hidden : (half + 1) * hidden] = (
                gate / (1.0 + jnp.exp(-gate)) * up
            ).astype(jnp.bfloat16)
        if k == 0:
            weights[4].wait()
            weights[5].wait()

        @pl.loop(0, width // block)
        def _(c, k=k, n=n):
            columns = pl.ds(pl.multiple_of(c * block, block), block)
            part = jnp.dot(act[:n], downs[:, columns], preferred_element_type=jnp.float32)
            results[k, :n, columns] = part.astype(jnp.bfloat16)

        stores[k].start()
    for copy in stores:
        copy.wait()


def expert_rows(xs, weights, step=256):
    width = xs[0].shape[1]
    hidden = weights[0].shape[1]
    tokens = sum(x.shape[0] for x in xs)
    step = min(step, max(x.shape[0] for x in xs))
    parts = sum(-(-x.shape[0] // step) for x in xs)
    far = pl.BlockSpec(memory_space=pltpu.HBM)
    return pl.pallas_call(
        lambda *refs: ffn_kernel(len(xs), refs),
        in_specs=[far] * (len(xs) + 6),
        out_specs=[far] * len(xs),
        out_shape=[jax.ShapeDtypeStruct(x.shape, jnp.bfloat16) for x in xs],
        scratch_shapes=[
            pltpu.VMEM((parts, step, width), jnp.bfloat16),
            pltpu.VMEM((4, width, hidden), jnp.bfloat16),
            pltpu.VMEM((2 * hidden, width), jnp.bfloat16),
            pltpu.VMEM((parts, step, width), jnp.bfloat16),
            pltpu.VMEM((step, 2 * hidden), jnp.bfloat16),
            pltpu.SemaphoreType.DMA((6,)),
            pltpu.SemaphoreType.DMA((parts,)),
            pltpu.SemaphoreType.DMA((parts,)),
        ],
        compiler_params=pltpu.CompilerParams(vmem_limit_bytes=60 * 1024 * 1024),
        cost_estimate=pl.CostEstimate(
            flops=12 * tokens * width * hidden,
            bytes_accessed=12 * width * hidden + 4 * tokens * width,
            transcendentals=2 * tokens * hidden,
        ),
        name="expert_rows",
    )(*xs, *weights)


def slot_kernel(hidden, router, ids, slots, out, places):
    experts = router.shape[1]
    tokens, capacity = hidden.shape[0], slots // experts
    logits = jnp.dot(hidden[...], router[...], preferred_element_type=jnp.float32)
    column = lax.broadcasted_iota(jnp.int32, (tokens, experts), 1)
    onehot = jnp.where(ids[...] == column, 1.0, 0.0)
    gate_score = 1.0 / (1.0 + jnp.exp(-jnp.sum(logits * onehot, axis=1, keepdims=True)))
    row = lax.broadcasted_iota(jnp.int32, (tokens, tokens), 0)
    earlier = lax.broadcasted_iota(jnp.int32, (tokens, tokens), 1)
    upto = jnp.where(earlier <= row, 1.0, 0.0).astype(jnp.bfloat16)
    counts = jnp.dot(upto, onehot.astype(jnp.bfloat16), preferred_element_type=jnp.float32)
    rank = jnp.sum(counts * onehot, axis=1, keepdims=True) - 1.0
    slot = ids[...] * capacity + rank.astype(jnp.int32)
    target = lax.broadcasted_iota(jnp.int32, (tokens, slots), 1)
    place = jnp.where(slot == target, 1.0, 0.0).astype(jnp.bfloat16)
    places[...] = place
    scaled = (hidden[...].astype(jnp.float32) * gate_score).astype(jnp.bfloat16)
    out[...] = lax.dot_general(
        place, scaled, (((0,), (0,)), ((), ())), preferred_element_type=jnp.float32
    ).astype(jnp.bfloat16)


def fill_slots(hidden, router, expert_ids, slots):
    tokens, width = hidden.shape
    outs = [
        jax.ShapeDtypeStruct((slots, width), jnp.bfloat16),
        jax.ShapeDtypeStruct((tokens, slots), jnp.bfloat16),
    ]

    def kernel(a, b, c, out, places):
        slot_kernel(a, b, c, slots, out, places)

    call = small(kernel, outs, "fill_slots", 1 << 20)
    return call(in_specs=[WHOLE] * 3, out_specs=[WHOLE] * 2)(hidden, router, expert_ids)


def route_experts(hidden, router, expert_ids, w_gate, w_up, w_down, exchanged, attend_rows):
    expert_table = router.shape[1]
    local_tokens = hidden.shape[0]
    model_width = hidden.shape[1]
    capacity = max(2, 2 * local_tokens // expert_table)
    exp_count = lax.axis_size("exp")
    own = (w_gate[0], w_up[0], w_down[0])
    other = tuple(lax.ppermute(w, "ctx", CORE_SWAP) for w in own)
    outgoing, places = fill_slots(hidden, router, expert_ids, expert_table * capacity)
    incoming = lax.all_to_all(
        outgoing.reshape(exp_count, capacity, model_width),
        "exp",
        split_axis=0,
        concat_axis=0,
        tiled=True,
    )
    rows = lax.all_gather(
        incoming.reshape(-1, model_width), "ctx", axis=0, tiled=True, axis_index_groups=RINGS
    )
    rows, exchanged = lax.optimization_barrier((rows, exchanged))
    (partial,) = expert_rows([rows], own + other)
    summed_output = lax.psum_scatter(
        partial, "ctx", scatter_dimension=0, tiled=True, axis_index_groups=RINGS
    )
    attention = attend_rows(*exchanged)
    summed_output, attention = lax.optimization_barrier((summed_output, attention))
    returned = lax.all_to_all(
        summed_output.reshape(exp_count, capacity, model_width),
        "exp",
        split_axis=0,
        concat_axis=0,
        tiled=True,
    )
    moe_out = jnp.dot(
        places, returned.reshape(-1, model_width), preferred_element_type=jnp.float32
    ).astype(jnp.bfloat16)
    return attention, moe_out


def shards(
    queries,
    key_states,
    value_state_rows,
    block_lists,
    hidden,
    router,
    expert_ids,
    w_gate,
    w_up,
    w_down,
):
    where, state, qs, rs = exchange_rows(queries, key_states, value_state_rows, block_lists)
    attention, moe_out = route_experts(
        hidden,
        router,
        expert_ids,
        w_gate,
        w_up,
        w_down,
        (qs, rs),
        lambda qs, rs: attend_all(where, state, qs, rs),
    )
    return (attention, moe_out)


def solution(mesh):
    placed = (
        P(None, ("ctx", "exp"), None),
        P(None, ("ctx", "exp"), None),
        P(None, ("ctx", "exp"), None),
        P(),
        P(("ctx", "exp"), None),
        P(),
        P(("ctx", "exp"), None),
        P("exp", None, "ctx"),
        P("exp", None, "ctx"),
        P("exp", "ctx", None),
    )
    return jax.shard_map(
        shards,
        mesh=mesh,
        in_specs=placed,
        out_specs=(P(None, ("ctx", "exp"), None), P(("ctx", "exp"), None)),
        check_vma=False,
    )
```

```python
import functools

import jax
import jax.numpy as jnp
from jax import lax
from jax.experimental import pallas as pl
from jax.experimental.pallas import tpu as pltpu
from jax.sharding import PartitionSpec as P

HEAD_DIM = 128
NEGATIVE_LARGE = -1e30
SIDE = 4
RINGS = [[2 * z + c for z in range(8)] for c in range(2)]
CORE_SWAP = [(i, i ^ 1) for i in range(16)]


def shift_x(d):
    return [(4 * a + b, 4 * ((a + d) % 4) + b) for a in range(4) for b in range(4)]


def shift_y(d):
    return [(4 * a + b, 4 * a + (b + d) % 4) for a in range(4) for b in range(4)]


def ordinary(vmem=48):
    return pltpu.CompilerParams(
        dimension_semantics=("arbitrary",), vmem_limit_bytes=vmem * 1024 * 1024
    )


WHOLE = pl.BlockSpec(memory_space=pltpu.VMEM)
TABLE = pl.BlockSpec(memory_space=pltpu.SMEM)


def small(kernel, outs, name, moved, scratch=()):
    return functools.partial(
        pl.pallas_call,
        kernel,
        out_shape=outs,
        scratch_shapes=scratch,
        compiler_params=pltpu.CompilerParams(vmem_limit_bytes=16 * 1024 * 1024),
        cost_estimate=pl.CostEstimate(flops=0, bytes_accessed=moved, transcendentals=0),
        name=name,
    )


def pair_kernel(keys, values, out):
    for h in range(SIDE):
        out[:, :, h * 256 : h * 256 + 128] = keys[:, :, h * 128 : h * 128 + 128]
        out[:, :, h * 256 + 128 : h * 256 + 256] = values[:, :, h * 128 : h * 128 + 128]


def pair_rows(keys, values):
    shape = keys.shape[:2] + (2 * keys.shape[2],)
    call = small(pair_kernel, jax.ShapeDtypeStruct(shape, keys.dtype), "pair_rows", 1 << 19)
    return call(in_specs=[WHOLE] * 2, out_specs=WHOLE)(keys, values)


def ring(d):
    return [(2 * z + c, 2 * ((z + d) % 8) + c) for z in range(8) for c in range(2)]


def up_z(v):
    return lax.ppermute(v, "ctx", ring(1))


def down_z(v):
    return lax.ppermute(v, "ctx", ring(-1))


def choose_kernel(table, *refs):
    own, b1, b2, b3, far_low, far_high, a3, a2, a1, mine, theirs, held = refs
    for k, block in ((0, own), (1, b1), (2, b2), (3, b3), (5, a3), (6, a2), (7, a1)):
        held[2 * k] = block[0]
        held[2 * k + 1] = block[1]
    held[8] = far_low[0]
    held[9] = far_high[0]
    for i in range(2):
        mine[i] = held[table[i]]
        theirs[i] = held[table[2 + i]]


def pass_blocks(paired):
    below, above = [paired], [paired]
    for _ in range(3):
        below.append(up_z(below[-1]))
        above.append(down_z(above[-1]))
    return below, above


def choose_blocks(below, above, table):
    paired = below[0]
    far_low, far_high = up_z(below[3][:1]), down_z(above[3][1:])
    out = jax.ShapeDtypeStruct(paired.shape, paired.dtype)
    held = pltpu.VMEM((16,) + paired.shape[1:], paired.dtype)
    call = small(choose_kernel, [out, out], "choose_blocks", 3 << 20, [held])
    return call(in_specs=[TABLE] + [WHOLE] * 9, out_specs=[WHOLE] * 2)(
        table, paired, *below[1:], far_low, far_high, above[3], above[2], above[1]
    )


def pick_kernel(table, own, mine, swapped, *outs):
    x = table[0]
    for d in range(SIDE):
        h = lax.rem(x + d, SIDE)
        columns = pl.ds(pl.multiple_of(h * 256, 256), 256)
        outs[d][0:2] = own[:, :, columns]
        for i in range(2):
            here = table[1 + i] > 0
            outs[d][2 + i] = jnp.where(here, mine[i, :, columns], swapped[i, :, columns])


def pick_heads(own, mine, swapped, table):
    rows = own.shape[1]
    part = jax.ShapeDtypeStruct((4, rows, 256), own.dtype)
    call = small(pick_kernel, [part] * SIDE, "pick_heads", 2 << 20)
    return call(in_specs=[TABLE] + [WHOLE] * 3, out_specs=[WHOLE] * SIDE)(
        table, own, mine, swapped
    )


def split_kernel(where, source, *outs):
    x = where[0]
    width = outs[0].shape[2]
    for d in range(SIDE):
        h = lax.rem(x + d, SIDE)
        outs[d][...] = source[:, :, pl.ds(pl.multiple_of(h * width, 128), width)]


def split_queries(queries, where):
    part = jax.ShapeDtypeStruct(queries.shape[:2] + (queries.shape[2] // SIDE,), queries.dtype)
    return pl.pallas_call(
        split_kernel,
        grid_spec=pltpu.PrefetchScalarGridSpec(
            num_scalar_prefetch=1,
            grid=(1,),
            in_specs=[pl.BlockSpec(queries.shape, lambda i, t: (0, 0, 0))],
            out_specs=[pl.BlockSpec(part.shape, lambda i, t: (0, 0, 0))] * SIDE,
        ),
        out_shape=[part] * SIDE,
        compiler_params=ordinary(16),
        cost_estimate=pl.CostEstimate(flops=0, bytes_accessed=1310720, transcendentals=0),
        name="split_queries",
    )(where, queries)


def stack_kernel(where, *refs):
    x = where[0]
    out = refs[SIDE]
    for d in range(SIDE):
        out[lax.rem(x + SIDE - d, SIDE)] = refs[d][...]


def stack_sources(parts, where):
    shape = parts[0].shape
    zeros = (0,) * len(shape)
    return pl.pallas_call(
        stack_kernel,
        grid_spec=pltpu.PrefetchScalarGridSpec(
            num_scalar_prefetch=1,
            grid=(1,),
            in_specs=[pl.BlockSpec(shape, lambda i, t: zeros)] * SIDE,
            out_specs=pl.BlockSpec((SIDE,) + shape, lambda i, t: (0,) + zeros),
        ),
        out_shape=jax.ShapeDtypeStruct((SIDE,) + shape, parts[0].dtype),
        compiler_params=ordinary(16),
        cost_estimate=pl.CostEstimate(flops=0, bytes_accessed=1 << 20, transcendentals=0),
        name="stack_sources",
    )(where, *parts)


def join_kernel(where, *refs):
    x = where[0]
    out = refs[SIDE]
    width = refs[0].shape[2]
    for d in range(SIDE):
        h = lax.rem(x + d, SIDE)
        out[:, :, pl.ds(pl.multiple_of(h * width, 128), width)] = refs[d][...]


def join_heads(parts, where):
    shape = parts[0].shape
    full = shape[:2] + (shape[2] * SIDE,)
    return pl.pallas_call(
        join_kernel,
        grid_spec=pltpu.PrefetchScalarGridSpec(
            num_scalar_prefetch=1,
            grid=(1,),
            in_specs=[pl.BlockSpec(shape, lambda i, t: (0, 0, 0))] * SIDE,
            out_specs=pl.BlockSpec(full, lambda i, t: (0, 0, 0)),
        ),
        out_shape=jax.ShapeDtypeStruct(full, parts[0].dtype),
        compiler_params=ordinary(16),
        cost_estimate=pl.CostEstimate(flops=0, bytes_accessed=1310720, transcendentals=0),
        name="join_heads",
    )(where, *parts)


NT = (((1,), (1,)), ((), ()))


def attend_kernel(where, q0, q1, q2, q3, r0, r1, r2, r3a, r3b, o0, o1, o2, o3, kown, vown, klist, vlist, qall, oall):
    p = pl.program_id(0)
    x, y, usable = where[0], where[1], where[2 + p]
    pieces = (r0, r1, r2)
    for xs in range(SIDE):
        last = r3a if xs < 2 else r3b
        for turn in range(SIDE):
            piece = pieces[turn][xs] if turn < 3 else last[xs % 2]
            at = pl.ds(xs * 256 + turn * 64, 64)
            kown[at, :] = piece[0, 0, :, :HEAD_DIM]
            vown[at, :] = piece[0, 0, :, HEAD_DIM:]
            klist[at, :] = piece[1, 0, :, :HEAD_DIM]
            vlist[at, :] = piece[1, 0, :, HEAD_DIM:]
    scaling = HEAD_DIM ** (-0.5)
    group = q0.shape[2] // HEAD_DIM
    rows = 64 * group
    qs, outs = (q0, q1, q2, q3), (o0, o1, o2, o3)
    query_row = lax.rem(lax.broadcasted_iota(jnp.int32, (rows, 256), 0), 64)
    key_index = lax.broadcasted_iota(jnp.int32, (rows, 256), 1)
    turn = key_index // 64
    behind = jnp.where(turn == 0, 0, jnp.where(turn == 1, 3, jnp.where(turn == 2, 1, 2)))
    key_pos = lax.rem(y + behind, SIDE) * 64 + lax.rem(key_index, 64)
    diagonal = key_pos <= y * 64 + query_row
    for d in range(SIDE):
        qall[lax.rem(x + SIDE - d, SIDE)] = qs[d][0]
    for case in range(SIDE):
        query = jnp.concatenate(
            [qall[case, :, g * HEAD_DIM : (g + 1) * HEAD_DIM] for g in range(group)], axis=0
        )
        before = case * 256
        own = lax.dot_general(
            query, kown[pl.ds(before, 256), :], NT, preferred_element_type=jnp.float32
        )
        own = jnp.where(diagonal, own * scaling, NEGATIVE_LARGE)
        far = lax.dot_general(query, klist[...], NT, preferred_element_type=jnp.float32)
        far = jnp.where(usable > 0, far * scaling, NEGATIVE_LARGE)
        top = jnp.maximum(jnp.max(own, axis=1, keepdims=True), jnp.max(far, axis=1, keepdims=True))
        if case:
            near = lax.dot_general(
                query, kown[pl.ds(0, before), :], NT, preferred_element_type=jnp.float32
            )
            near = near * scaling
            top = jnp.maximum(top, jnp.max(near, axis=1, keepdims=True))
        own = jnp.exp(own - top)
        far = jnp.exp(far - top)
        total = jnp.sum(own, axis=1, keepdims=True) + jnp.sum(far, axis=1, keepdims=True)
        mixed = jnp.dot(
            own.astype(jnp.bfloat16), vown[pl.ds(before, 256), :], preferred_element_type=jnp.float32
        ) + jnp.dot(far.astype(jnp.bfloat16), vlist[...], preferred_element_type=jnp.float32)
        if case:
            near = jnp.exp(near - top)
            total = total + jnp.sum(near, axis=1, keepdims=True)
            mixed = mixed + jnp.dot(
                near.astype(jnp.bfloat16),
                vown[pl.ds(0, before), :],
                preferred_element_type=jnp.float32,
            )
        mixed = (mixed / total).astype(jnp.bfloat16)
        for g in range(group):
            oall[case, :, g * HEAD_DIM : (g + 1) * HEAD_DIM] = mixed[g * 64 : (g + 1) * 64]
    for d in range(SIDE):
        outs[d][0] = oall[lax.rem(x + SIDE - d, SIDE)]


def attend(where, qs, rs):
    qspec = pl.BlockSpec((1,) + qs[0].shape[1:], lambda i, t: (i, 0, 0))

    def rspec(r):
        return pl.BlockSpec((r.shape[0], 2, 1) + r.shape[3:], lambda i, t: (0, 0, i, 0, 0))

    return pl.pallas_call(
        attend_kernel,
        grid_spec=pltpu.PrefetchScalarGridSpec(
            num_scalar_prefetch=1,
            grid=(2,),
            in_specs=[qspec] * SIDE + [rspec(r) for r in rs],
            out_specs=[qspec] * SIDE,
            scratch_shapes=[pltpu.VMEM((1024, HEAD_DIM), jnp.bfloat16)] * 4
            + [pltpu.VMEM((SIDE,) + qs[0].shape[1:], jnp.bfloat16)] * 2,
        ),
        out_shape=[jax.ShapeDtypeStruct(q.shape, q.dtype) for q in qs],
        compiler_params=ordinary(40),
        cost_estimate=pl.CostEstimate(
            flops=2200000000, bytes_accessed=4 << 20, transcendentals=4300000
        ),
        name="attend",
    )(where, *qs, *rs)


def exchange_rows(queries, below, above, block_lists):
    ctx_count = lax.axis_size("ctx")
    blocks_total = 2 * ctx_count
    ctx_index = lax.axis_index("ctx")
    exp_index = lax.axis_index("exp")
    x, y = lax.div(exp_index, SIDE), lax.rem(exp_index, SIDE)
    z, core = lax.div(ctx_index, 2), lax.rem(ctx_index, 2)
    where = jnp.stack([x, y]).astype(jnp.int32)
    other = ctx_index + 1 - 2 * core
    own_blocks = jnp.stack(
        [ctx_index, blocks_total - 1 - ctx_index, other, blocks_total - 1 - other]
    )
    listed = block_lists[own_blocks]
    usable = (listed != own_blocks).astype(jnp.int32)
    holder = jnp.minimum(listed, blocks_total - 1 - listed)
    distance = lax.rem(z + 8 - lax.div(holder, 2), 8)
    chosen = (2 * distance + (listed >= ctx_count).astype(jnp.int32)).astype(jnp.int32)
    local = (lax.rem(holder, 2) == core).astype(jnp.int32)

    paired = below[0]
    mine, theirs = choose_blocks(below, above, chosen)
    swapped = lax.ppermute(theirs, "ctx", CORE_SWAP)
    picked = pick_heads(
        paired, mine, swapped, jnp.concatenate([x[None], local[:2]]).astype(jnp.int32)
    )
    split = split_queries(queries, where)
    qs = [split[0]] + [lax.ppermute(split[d], "exp", shift_x(d)) for d in range(1, SIDE)]
    received = [picked[0]] + [lax.ppermute(picked[d], "exp", shift_x(d)) for d in range(1, SIDE)]
    r0 = stack_sources(received, where)
    r1 = lax.ppermute(r0, "exp", shift_y(1))
    r2 = lax.ppermute(r0, "exp", shift_y(-1))
    r3a = lax.ppermute(r1[:2], "exp", shift_y(1))
    r3b = lax.ppermute(r2[2:], "exp", shift_y(-1))
    rs = [r.reshape((r.shape[0], 2, 2) + r.shape[2:]) for r in (r0, r1, r2, r3a, r3b)]
    return where, jnp.concatenate([where, usable[:2]]), qs, rs


def attend_all(where, state, qs, rs):
    outs = attend(state, qs, rs)
    back = [outs[0]] + [lax.ppermute(outs[d], "exp", shift_x(-d)) for d in range(1, SIDE)]
    return join_heads(back, where)


def ffn_kernel(counts, refs):
    xs, ws, outs = refs[:counts], refs[counts : counts + 6], refs[counts + 6 : 2 * counts + 6]
    rows, gates, downs, results, act, w_sem, x_sem, o_sem = refs[2 * counts + 6 :]
    width, hidden = gates.shape[1], gates.shape[2]
    step = rows.shape[1]
    parts = []
    for x, out in zip(xs, outs):
        for at in range(0, x.shape[0], step):
            parts.append((x, out, at, min(step, x.shape[0] - at)))
    loads = [
        pltpu.make_async_copy(
            x.at[pl.ds(at, n), :], rows.at[k, pl.ds(0, n), :], x_sem.at[k]
        )
        for k, (x, _, at, n) in enumerate(parts)
    ]
    stores = [
        pltpu.make_async_copy(
            results.at[k, pl.ds(0, n), :], out.at[pl.ds(at, n), :], o_sem.at[k]
        )
        for k, (_, out, at, n) in enumerate(parts)
    ]
    targets = [gates.at[0], gates.at[1], gates.at[2], gates.at[3]]
    targets += [downs.at[pl.ds(0, hidden), :], downs.at[pl.ds(hidden, hidden), :]]
    order = (0, 1, 3, 4, 2, 5)
    weights = [pltpu.make_async_copy(ws[w], targets[k], w_sem.at[k]) for k, w in enumerate(order)]
    loads[0].start()
    for copy in weights:
        copy.start()
    for copy in loads[1:]:
        copy.start()
    block = 1024
    for k, (x, out, at, n) in enumerate(parts):
        loads[k].wait()
        for half in range(2):
            if k == 0:
                weights[2 * half].wait()
            gate = jnp.dot(rows[k, :n], gates[2 * half], preferred_element_type=jnp.float32)
            if k == 0:
                weights[2 * half + 1].wait()
            up = jnp.dot(rows[k, :n], gates[2 * half + 1], preferred_element_type=jnp.float32)
            act[:n, half * hidden : (half + 1) * hidden] = (
                gate / (1.0 + jnp.exp(-gate)) * up
            ).astype(jnp.bfloat16)
        if k == 0:
            weights[4].wait()
            weights[5].wait()

        @pl.loop(0, width // block)
        def _(c, k=k, n=n):
            columns = pl.ds(pl.multiple_of(c * block, block), block)
            part = jnp.dot(act[:n], downs[:, columns], preferred_element_type=jnp.float32)
            results[k, :n, columns] = part.astype(jnp.bfloat16)

        stores[k].start()
    for copy in stores:
        copy.wait()


def expert_rows(xs, weights, step=512):
    width = xs[0].shape[1]
    hidden = weights[0].shape[1]
    tokens = sum(x.shape[0] for x in xs)
    step = min(step, max(x.shape[0] for x in xs))
    parts = sum(-(-x.shape[0] // step) for x in xs)
    far = pl.BlockSpec(memory_space=pltpu.HBM)
    return pl.pallas_call(
        lambda *refs: ffn_kernel(len(xs), refs),
        in_specs=[far] * (len(xs) + 6),
        out_specs=[far] * len(xs),
        out_shape=[jax.ShapeDtypeStruct(x.shape, jnp.bfloat16) for x in xs],
        scratch_shapes=[
            pltpu.VMEM((parts, step, width), jnp.bfloat16),
            pltpu.VMEM((4, width, hidden), jnp.bfloat16),
            pltpu.VMEM((2 * hidden, width), jnp.bfloat16),
            pltpu.VMEM((parts, step, width), jnp.bfloat16),
            pltpu.VMEM((step, 2 * hidden), jnp.bfloat16),
            pltpu.SemaphoreType.DMA((6,)),
            pltpu.SemaphoreType.DMA((parts,)),
            pltpu.SemaphoreType.DMA((parts,)),
        ],
        compiler_params=pltpu.CompilerParams(vmem_limit_bytes=60 * 1024 * 1024),
        cost_estimate=pl.CostEstimate(
            flops=12 * tokens * width * hidden,
            bytes_accessed=12 * width * hidden + 4 * tokens * width,
            transcendentals=2 * tokens * hidden,
        ),
        name="expert_rows",
    )(*xs, *weights)


def slot_kernel(hidden, router, ids, out, places):
    experts, tokens, slots = router.shape[0], hidden.shape[0], out.shape[0]
    logits = lax.dot_general(router[...], hidden[...], NT, preferred_element_type=jnp.float32)
    named = ids[...] == lax.broadcasted_iota(jnp.int32, (experts, tokens), 0)
    onehot = jnp.where(named, 1.0, 0.0)
    gate_row = 1.0 / (1.0 + jnp.exp(-jnp.sum(logits * onehot, axis=0, keepdims=True)))
    row = lax.broadcasted_iota(jnp.int32, (tokens, tokens), 0)
    column = lax.broadcasted_iota(jnp.int32, (tokens, tokens), 1)
    upto = jnp.where(row <= column, 1.0, 0.0).astype(jnp.bfloat16)
    counts = jnp.dot(onehot.astype(jnp.bfloat16), upto, preferred_element_type=jnp.float32)
    rank = jnp.sum(counts * onehot, axis=0, keepdims=True) - 1.0
    slot = ids[...] * (slots // experts) + rank.astype(jnp.int32)
    target = lax.broadcasted_iota(jnp.int32, (slots, tokens), 0)
    place = jnp.where(slot == target, 1.0, 0.0).astype(jnp.bfloat16)
    places[...] = place
    gate_score = jnp.sum(jnp.where(row == column, gate_row, 0.0), axis=1, keepdims=True)
    scaled = (hidden[...].astype(jnp.float32) * gate_score).astype(jnp.bfloat16)
    out[...] = jnp.dot(place, scaled, preferred_element_type=jnp.float32).astype(jnp.bfloat16)


def fill_slots(hidden, router, expert_ids, slots):
    tokens, width = hidden.shape
    outs = [
        jax.ShapeDtypeStruct((slots, width), jnp.bfloat16),
        jax.ShapeDtypeStruct((slots, tokens), jnp.bfloat16),
    ]
    call = small(slot_kernel, outs, "fill_slots", 1 << 20)
    return call(in_specs=[WHOLE] * 3, out_specs=[WHOLE] * 2)(hidden, router.T, expert_ids.T)


def send_tokens(hidden, router, expert_ids):
    expert_table = router.shape[1]
    local_tokens = hidden.shape[0]
    model_width = hidden.shape[1]
    capacity = max(2, 2 * local_tokens // expert_table)
    exp_count = lax.axis_size("exp")
    outgoing, places = fill_slots(hidden, router, expert_ids, expert_table * capacity)
    incoming = lax.all_to_all(
        outgoing.reshape(exp_count, capacity, model_width),
        "exp",
        split_axis=0,
        concat_axis=0,
        tiled=True,
    )
    return incoming.reshape(-1, model_width), places


def route_experts(incoming, places, w_gate, w_up, w_down, exchanged, attend_rows):
    model_width = incoming.shape[1]
    exp_count = lax.axis_size("exp")
    own = (w_gate[0], w_up[0], w_down[0])
    other = tuple(lax.ppermute(w, "ctx", CORE_SWAP) for w in own)
    rows = lax.all_gather(
        incoming, "ctx", axis=0, tiled=True, axis_index_groups=RINGS
    )
    rows, exchanged = lax.optimization_barrier((rows, exchanged))
    (partial,) = expert_rows([rows], own + other)
    summed_output = lax.psum_scatter(
        partial, "ctx", scatter_dimension=0, tiled=True, axis_index_groups=RINGS
    )
    attention = attend_rows(*exchanged)
    summed_output, attention = lax.optimization_barrier((summed_output, attention))
    returned = lax.all_to_all(
        summed_output.reshape(exp_count, -1, model_width),
        "exp",
        split_axis=0,
        concat_axis=0,
        tiled=True,
    )
    moe_out = lax.dot_general(
        places,
        returned.reshape(-1, model_width),
        (((0,), (0,)), ((), ())),
        preferred_element_type=jnp.float32,
    ).astype(jnp.bfloat16)
    return attention, moe_out


def shards(
    queries,
    key_states,
    value_state_rows,
    block_lists,
    hidden,
    router,
    expert_ids,
    w_gate,
    w_up,
    w_down,
):
    below, above = pass_blocks(pair_rows(key_states, value_state_rows))
    incoming, places = send_tokens(hidden, router, expert_ids)
    incoming, below, above = lax.optimization_barrier((incoming, below, above))
    where, state, qs, rs = exchange_rows(queries, below, above, block_lists)
    attention, moe_out = route_experts(
        incoming,
        places,
        w_gate,
        w_up,
        w_down,
        (qs, rs),
        lambda qs, rs: attend_all(where, state, qs, rs),
    )
    return (attention, moe_out)


def solution(mesh):
    placed = (
        P(None, ("ctx", "exp"), None),
        P(None, ("ctx", "exp"), None),
        P(None, ("ctx", "exp"), None),
        P(),
        P(("ctx", "exp"), None),
        P(),
        P(("ctx", "exp"), None),
        P("exp", None, "ctx"),
        P("exp", None, "ctx"),
        P("exp", "ctx", None),
    )
    return jax.shard_map(
        shards,
        mesh=mesh,
        in_specs=placed,
        out_specs=(P(None, ("ctx", "exp"), None), P(("ctx", "exp"), None)),
        check_vma=False,
    )
```

```python
import functools

import jax
import jax.numpy as jnp
from jax import lax
from jax.experimental import pallas as pl
from jax.experimental.pallas import tpu as pltpu
from jax.sharding import PartitionSpec as P

HEAD_DIM = 128
NEGATIVE_LARGE = -1e30
SIDE = 4
RINGS = [[2 * z + c for z in range(8)] for c in range(2)]
CORE_SWAP = [(i, i ^ 1) for i in range(16)]


def ordinary(vmem=48):
    return pltpu.CompilerParams(
        dimension_semantics=("arbitrary",), vmem_limit_bytes=vmem * 1024 * 1024
    )


WHOLE = pl.BlockSpec(memory_space=pltpu.VMEM)
TABLE = pl.BlockSpec(memory_space=pltpu.SMEM)


def small(kernel, outs, name, moved, scratch=()):
    return functools.partial(
        pl.pallas_call,
        kernel,
        out_shape=outs,
        scratch_shapes=scratch,
        compiler_params=pltpu.CompilerParams(vmem_limit_bytes=16 * 1024 * 1024),
        cost_estimate=pl.CostEstimate(flops=0, bytes_accessed=moved, transcendentals=0),
        name=name,
    )


def pair_kernel(keys, values, out):
    for h in range(SIDE):
        out[:, :, h * 256 : h * 256 + 128] = keys[:, :, h * 128 : h * 128 + 128]
        out[:, :, h * 256 + 128 : h * 256 + 256] = values[:, :, h * 128 : h * 128 + 128]


def pair_rows(keys, values):
    shape = keys.shape[:2] + (2 * keys.shape[2],)
    call = small(pair_kernel, jax.ShapeDtypeStruct(shape, keys.dtype), "pair_rows", 1 << 19)
    return call(in_specs=[WHOLE] * 2, out_specs=WHOLE)(keys, values)


def ring(d):
    return [(2 * z + c, 2 * ((z + d) % 8) + c) for z in range(8) for c in range(2)]


def up_z(v):
    return lax.ppermute(v, "ctx", ring(1))


def down_z(v):
    return lax.ppermute(v, "ctx", ring(-1))


def choose_kernel(table, *refs):
    own, b1, b2, b3, far_low, far_high, a3, a2, a1, mine, theirs, held = refs
    for k, block in ((0, own), (1, b1), (2, b2), (3, b3), (5, a3), (6, a2), (7, a1)):
        held[2 * k] = block[0]
        held[2 * k + 1] = block[1]
    held[8] = far_low[0]
    held[9] = far_high[0]
    for i in range(2):
        mine[i] = held[table[i]]
        theirs[i] = held[table[2 + i]]


def choose_blocks(below, above, table):
    paired = below[0]
    far_low, far_high = up_z(below[3][:1]), down_z(above[3][1:])
    out = jax.ShapeDtypeStruct(paired.shape, paired.dtype)
    held = pltpu.VMEM((16,) + paired.shape[1:], paired.dtype)
    call = small(choose_kernel, [out, out], "choose_blocks", 3 << 20, [held])
    return call(in_specs=[TABLE] + [WHOLE] * 9, out_specs=[WHOLE] * 2)(
        table, paired, *below[1:], far_low, far_high, above[3], above[2], above[1]
    )


def pack_own_kernel(own, queries, out):
    group = queries.shape[2] // (SIDE * HEAD_DIM)
    for h in range(SIDE):
        at = h * 256
        for y in range(SIDE):
            to = SIDE * h + y
            for b in range(2):
                out[to, b * 128 : b * 128 + 64] = own[b, :, at : at + 128]
                out[to, b * 128 + 64 : b * 128 + 128] = own[b, :, at + 128 : at + 256]
                for g in range(group):
                    row = 256 + (b * group + g) * 16
                    column = (h * group + g) * HEAD_DIM
                    out[to, row : row + 16] = queries[
                        b, 16 * y : 16 * y + 16, column : column + HEAD_DIM
                    ]


def pack_own(own, queries):
    rows = 256 + 2 * 16 * queries.shape[2] // (SIDE * HEAD_DIM)
    out = jax.ShapeDtypeStruct((SIDE * SIDE, rows, HEAD_DIM), own.dtype)
    call = small(pack_own_kernel, out, "pack_own", 3 << 20)
    return call(in_specs=[WHOLE] * 2, out_specs=WHOLE)(own, queries)


def pack_listed_kernel(table, mine, swapped, out):
    for h in range(SIDE):
        at = h * 256
        for b in range(2):
            piece = jnp.where(
                table[b] > 0, mine[b, :, at : at + 256], swapped[b, :, at : at + 256]
            )
            for y in range(SIDE):
                out[SIDE * h + y, b * 128 : b * 128 + 64] = piece[:, :HEAD_DIM]
                out[SIDE * h + y, b * 128 + 64 : b * 128 + 128] = piece[:, HEAD_DIM:]


def pack_listed(table, mine, swapped):
    out = jax.ShapeDtypeStruct((SIDE * SIDE, 256, HEAD_DIM), mine.dtype)
    call = small(pack_listed_kernel, out, "pack_listed", 3 << 20)
    return call(in_specs=[TABLE] + [WHOLE] * 2, out_specs=WHOLE)(table, mine, swapped)


def unpack_kernel(back, out):
    group = out.shape[2] // (SIDE * HEAD_DIM)
    for h in range(SIDE):
        for y in range(SIDE):
            for p in range(2):
                for g in range(group):
                    row = (p * group + g) * 16
                    column = (h * group + g) * HEAD_DIM
                    out[p, 16 * y : 16 * y + 16, column : column + HEAD_DIM] = back[
                        SIDE * h + y, row : row + 16
                    ]


def unpack(back, shape):
    call = small(unpack_kernel, jax.ShapeDtypeStruct(shape, back.dtype), "unpack", 1310720)
    return call(in_specs=[WHOLE], out_specs=WHOLE)(back)


NT = (((1,), (1,)), ((), ()))


def attend_kernel(table, seen, listed, out, kown, vown, klist, vlist):
    p = pl.program_id(0)
    y, usable = table[0], table[1 + p]
    own_at = pl.multiple_of(p * 128, 128)
    for e in range(SIDE * SIDE):
        at = pl.ds(e * 64, 64)
        kown[at, :] = seen[e, pl.ds(own_at, 64), :]
        vown[at, :] = seen[e, pl.ds(own_at + 64, 64), :]
        klist[at, :] = listed[e, pl.ds(own_at, 64), :]
        vlist[at, :] = listed[e, pl.ds(own_at + 64, 64), :]
    scaling = HEAD_DIM ** (-0.5)
    group = out.shape[1] // 32
    rows = 64 * group
    row = lax.rem(lax.broadcasted_iota(jnp.int32, (rows, 256), 0), 64)
    query_pos = lax.div(row, 16) * 64 + 16 * y + lax.rem(row, 16)
    diagonal = lax.broadcasted_iota(jnp.int32, (rows, 256), 1) <= query_pos
    for case in range(SIDE):
        pieces = []
        for g in range(group):
            at = pl.multiple_of(256 + (p * group + g) * 16, 16)
            for e in range(SIDE):
                pieces.append(seen[SIDE * case + e, pl.ds(at, 16), :])
        query = jnp.concatenate(pieces, axis=0)
        before = case * 256
        own = lax.dot_general(
            query, kown[pl.ds(before, 256), :], NT, preferred_element_type=jnp.float32
        )
        own = jnp.where(diagonal, own * scaling, NEGATIVE_LARGE)
        far = lax.dot_general(query, klist[...], NT, preferred_element_type=jnp.float32)
        far = jnp.where(usable > 0, far * scaling, NEGATIVE_LARGE)
        top = jnp.maximum(jnp.max(own, axis=1, keepdims=True), jnp.max(far, axis=1, keepdims=True))
        if case:
            near = lax.dot_general(
                query, kown[pl.ds(0, before), :], NT, preferred_element_type=jnp.float32
            )
            near = near * scaling
            top = jnp.maximum(top, jnp.max(near, axis=1, keepdims=True))
        own = jnp.exp(own - top)
        far = jnp.exp(far - top)
        total = jnp.sum(own, axis=1, keepdims=True) + jnp.sum(far, axis=1, keepdims=True)
        mixed = jnp.dot(
            own.astype(jnp.bfloat16), vown[pl.ds(before, 256), :], preferred_element_type=jnp.float32
        ) + jnp.dot(far.astype(jnp.bfloat16), vlist[...], preferred_element_type=jnp.float32)
        if case:
            near = jnp.exp(near - top)
            total = total + jnp.sum(near, axis=1, keepdims=True)
            mixed = mixed + jnp.dot(
                near.astype(jnp.bfloat16),
                vown[pl.ds(0, before), :],
                preferred_element_type=jnp.float32,
            )
        mixed = (mixed / total).astype(jnp.bfloat16)
        for g in range(group):
            at = pl.multiple_of((p * group + g) * 16, 16)
            for e in range(SIDE):
                start = g * 64 + e * 16
                out[SIDE * case + e, pl.ds(at, 16), :] = mixed[start : start + 16]


def attend(table, seen, listed):
    rows = seen.shape[1] - 256
    out = jax.ShapeDtypeStruct((seen.shape[0], rows, seen.shape[2]), seen.dtype)
    zeros = lambda i, t: (0, 0, 0)
    return pl.pallas_call(
        attend_kernel,
        grid_spec=pltpu.PrefetchScalarGridSpec(
            num_scalar_prefetch=1,
            grid=(2,),
            in_specs=[pl.BlockSpec(seen.shape, zeros), pl.BlockSpec(listed.shape, zeros)],
            out_specs=pl.BlockSpec(out.shape, zeros),
            scratch_shapes=[pltpu.VMEM((1024, HEAD_DIM), jnp.bfloat16)] * 4,
        ),
        out_shape=out,
        compiler_params=ordinary(40),
        cost_estimate=pl.CostEstimate(
            flops=2200000000, bytes_accessed=4 << 20, transcendentals=4300000
        ),
        name="attend",
    )(table, seen, listed)


def exchange_rows(below, above, block_lists):
    ctx_count = lax.axis_size("ctx")
    blocks_total = 2 * ctx_count
    ctx_index = lax.axis_index("ctx")
    exp_index = lax.axis_index("exp")
    y = lax.rem(exp_index, SIDE)
    z, core = lax.div(ctx_index, 2), lax.rem(ctx_index, 2)
    other = ctx_index + 1 - 2 * core
    own_blocks = jnp.stack(
        [ctx_index, blocks_total - 1 - ctx_index, other, blocks_total - 1 - other]
    )
    listed = block_lists[own_blocks]
    usable = (listed != own_blocks).astype(jnp.int32)
    holder = jnp.minimum(listed, blocks_total - 1 - listed)
    distance = lax.rem(z + 8 - lax.div(holder, 2), 8)
    chosen = (2 * distance + (listed >= ctx_count).astype(jnp.int32)).astype(jnp.int32)
    local = (lax.rem(holder, 2) == core).astype(jnp.int32)

    mine, theirs = choose_blocks(below, above, chosen)
    swapped = lax.ppermute(theirs, "ctx", CORE_SWAP)
    packed = pack_listed(local[:2], mine, swapped)
    return packed, jnp.concatenate([y[None], usable[:2]]).astype(jnp.int32)


def trade(v):
    return lax.all_to_all(v, "exp", split_axis=0, concat_axis=0, tiled=True)


def ffn_kernel(counts, refs):
    xs, ws, outs = refs[:counts], refs[counts : counts + 6], refs[counts + 6 : 2 * counts + 6]
    rows, gates, downs, results, act, w_sem, x_sem, o_sem = refs[2 * counts + 6 :]
    width, hidden = gates.shape[1], gates.shape[2]
    step = rows.shape[1]
    parts = []
    for x, out in zip(xs, outs):
        for at in range(0, x.shape[0], step):
            parts.append((x, out, at, min(step, x.shape[0] - at)))
    loads = [
        pltpu.make_async_copy(
            x.at[pl.ds(at, n), :], rows.at[k, pl.ds(0, n), :], x_sem.at[k]
        )
        for k, (x, _, at, n) in enumerate(parts)
    ]
    stores = [
        pltpu.make_async_copy(
            results.at[k, pl.ds(0, n), :], out.at[pl.ds(at, n), :], o_sem.at[k]
        )
        for k, (_, out, at, n) in enumerate(parts)
    ]
    targets = [gates.at[0], gates.at[1], gates.at[2], gates.at[3]]
    targets += [downs.at[pl.ds(0, hidden), :], downs.at[pl.ds(hidden, hidden), :]]
    order = (0, 1, 3, 4, 2, 5)
    weights = [pltpu.make_async_copy(ws[w], targets[k], w_sem.at[k]) for k, w in enumerate(order)]
    loads[0].start()
    for copy in weights:
        copy.start()
    for copy in loads[1:]:
        copy.start()
    block = 1024
    for k, (x, out, at, n) in enumerate(parts):
        loads[k].wait()
        for half in range(2):
            if k == 0:
                weights[2 * half].wait()
            gate = jnp.dot(rows[k, :n], gates[2 * half], preferred_element_type=jnp.float32)
            if k == 0:
                weights[2 * half + 1].wait()
            up = jnp.dot(rows[k, :n], gates[2 * half + 1], preferred_element_type=jnp.float32)
            act[:n, half * hidden : (half + 1) * hidden] = (
                gate / (1.0 + jnp.exp(-gate)) * up
            ).astype(jnp.bfloat16)
        if k == 0:
            weights[4].wait()
            weights[5].wait()

        @pl.loop(0, width // block)
        def _(c, k=k, n=n):
            columns = pl.ds(pl.multiple_of(c * block, block), block)
            part = jnp.dot(act[:n], downs[:, columns], preferred_element_type=jnp.float32)
            results[k, :n, columns] = part.astype(jnp.bfloat16)

        stores[k].start()
    for copy in stores:
        copy.wait()


def expert_rows(xs, weights, step=256):
    width = xs[0].shape[1]
    hidden = weights[0].shape[1]
    tokens = sum(x.shape[0] for x in xs)
    step = min(step, max(x.shape[0] for x in xs))
    parts = sum(-(-x.shape[0] // step) for x in xs)
    far = pl.BlockSpec(memory_space=pltpu.HBM)
    return pl.pallas_call(
        lambda *refs: ffn_kernel(len(xs), refs),
        in_specs=[far] * (len(xs) + 6),
        out_specs=[far] * len(xs),
        out_shape=[jax.ShapeDtypeStruct(x.shape, jnp.bfloat16) for x in xs],
        scratch_shapes=[
            pltpu.VMEM((parts, step, width), jnp.bfloat16),
            pltpu.VMEM((4, width, hidden), jnp.bfloat16),
            pltpu.VMEM((2 * hidden, width), jnp.bfloat16),
            pltpu.VMEM((parts, step, width), jnp.bfloat16),
            pltpu.VMEM((step, 2 * hidden), jnp.bfloat16),
            pltpu.SemaphoreType.DMA((6,)),
            pltpu.SemaphoreType.DMA((parts,)),
            pltpu.SemaphoreType.DMA((parts,)),
        ],
        compiler_params=pltpu.CompilerParams(vmem_limit_bytes=60 * 1024 * 1024),
        cost_estimate=pl.CostEstimate(
            flops=12 * tokens * width * hidden,
            bytes_accessed=12 * width * hidden + 4 * tokens * width,
            transcendentals=2 * tokens * hidden,
        ),
        name="expert_rows",
    )(*xs, *weights)


def slot_kernel(hidden, router, ids, out, places):
    experts, tokens, slots = router.shape[0], hidden.shape[0], out.shape[0]
    logits = lax.dot_general(router[...], hidden[...], NT, preferred_element_type=jnp.float32)
    named = ids[...] == lax.broadcasted_iota(jnp.int32, (experts, tokens), 0)
    onehot = jnp.where(named, 1.0, 0.0)
    gate_row = 1.0 / (1.0 + jnp.exp(-jnp.sum(logits * onehot, axis=0, keepdims=True)))
    row = lax.broadcasted_iota(jnp.int32, (tokens, tokens), 0)
    column = lax.broadcasted_iota(jnp.int32, (tokens, tokens), 1)
    upto = jnp.where(row <= column, 1.0, 0.0).astype(jnp.bfloat16)
    counts = jnp.dot(onehot.astype(jnp.bfloat16), upto, preferred_element_type=jnp.float32)
    rank = jnp.sum(counts * onehot, axis=0, keepdims=True) - 1.0
    slot = ids[...] * (slots // experts) + rank.astype(jnp.int32)
    target = lax.broadcasted_iota(jnp.int32, (slots, tokens), 0)
    place = jnp.where(slot == target, 1.0, 0.0).astype(jnp.bfloat16)
    places[...] = place
    gate_score = jnp.sum(jnp.where(row == column, gate_row, 0.0), axis=1, keepdims=True)
    scaled = (hidden[...].astype(jnp.float32) * gate_score).astype(jnp.bfloat16)
    out[...] = jnp.dot(place, scaled, preferred_element_type=jnp.float32).astype(jnp.bfloat16)


def fill_slots(hidden, router, expert_ids, slots):
    tokens, width = hidden.shape
    outs = [
        jax.ShapeDtypeStruct((slots, width), jnp.bfloat16),
        jax.ShapeDtypeStruct((slots, tokens), jnp.bfloat16),
    ]
    call = small(slot_kernel, outs, "fill_slots", 1 << 20)
    return call(in_specs=[WHOLE] * 3, out_specs=[WHOLE] * 2)(hidden, router.T, expert_ids.T)


def route_experts(incoming, places, weights, seen, packed, state, shape):
    model_width = incoming.shape[1]
    exp_count = lax.axis_size("exp")
    rows = lax.all_gather(
        incoming, "ctx", axis=0, tiled=True, axis_index_groups=RINGS
    )
    rows, seen, packed = lax.optimization_barrier((rows, seen, packed))
    listed = trade(packed)
    (partial,) = expert_rows([rows], weights)
    summed_output = lax.psum_scatter(
        partial, "ctx", scatter_dimension=0, tiled=True, axis_index_groups=RINGS
    )
    attention = unpack(trade(attend(state, seen, listed)), shape)
    summed_output, attention = lax.optimization_barrier((summed_output, attention))
    returned = trade(summed_output.reshape(exp_count, -1, model_width))
    moe_out = lax.dot_general(
        places,
        returned.reshape(-1, model_width),
        (((0,), (0,)), ((), ())),
        preferred_element_type=jnp.float32,
    ).astype(jnp.bfloat16)
    return attention, moe_out


def shards(
    queries,
    key_states,
    value_state_rows,
    block_lists,
    hidden,
    router,
    expert_ids,
    w_gate,
    w_up,
    w_down,
):
    own = (w_gate[0], w_up[0], w_down[0])
    other = tuple(lax.ppermute(w, "ctx", CORE_SWAP) for w in own)
    experts, width = router.shape[1], router.shape[0]
    capacity = 2 * hidden.shape[0] // experts
    outgoing, places = fill_slots(hidden, router, expert_ids, experts * capacity)
    paired = pair_rows(key_states, value_state_rows)
    outgoing, paired = lax.optimization_barrier((outgoing, paired))
    incoming = trade(outgoing.reshape(experts, capacity, width)).reshape(-1, width)
    below, above = [paired, up_z(paired)], [paired, down_z(paired)]
    incoming, below[1], above[1] = lax.optimization_barrier((incoming, below[1], above[1]))
    for _ in range(2):
        below.append(up_z(below[-1]))
        above.append(down_z(above[-1]))
    seen = trade(pack_own(below[0], queries))
    packed, state = exchange_rows(below, above, block_lists)
    attention, moe_out = route_experts(
        incoming, places, own + other, seen, packed, state, queries.shape
    )
    return (attention, moe_out)


def solution(mesh):
    placed = (
        P(None, ("ctx", "exp"), None),
        P(None, ("ctx", "exp"), None),
        P(None, ("ctx", "exp"), None),
        P(),
        P(("ctx", "exp"), None),
        P(),
        P(("ctx", "exp"), None),
        P("exp", None, "ctx"),
        P("exp", None, "ctx"),
        P("exp", "ctx", None),
    )
    return jax.shard_map(
        shards,
        mesh=mesh,
        in_specs=placed,
        out_specs=(P(None, ("ctx", "exp"), None), P(("ctx", "exp"), None)),
        check_vma=False,
    )
```

```python
import functools

import jax
import jax.numpy as jnp
from jax import lax
from jax.experimental import pallas as pl
from jax.experimental.pallas import tpu as pltpu
from jax.sharding import PartitionSpec as P

HEAD_DIM = 128
NEGATIVE_LARGE = -1e30
SIDE = 4
RINGS = [[2 * z + c for z in range(8)] for c in range(2)]
CORE_SWAP = [(i, i ^ 1) for i in range(16)]


def ordinary(vmem=48):
    return pltpu.CompilerParams(
        dimension_semantics=("arbitrary",), vmem_limit_bytes=vmem * 1024 * 1024
    )


WHOLE = pl.BlockSpec(memory_space=pltpu.VMEM)
TABLE = pl.BlockSpec(memory_space=pltpu.SMEM)


def small(kernel, outs, name, moved, scratch=()):
    return functools.partial(
        pl.pallas_call,
        kernel,
        out_shape=outs,
        scratch_shapes=scratch,
        compiler_params=pltpu.CompilerParams(vmem_limit_bytes=16 * 1024 * 1024),
        cost_estimate=pl.CostEstimate(flops=0, bytes_accessed=moved, transcendentals=0),
        name=name,
    )


def pair_kernel(keys, values, out):
    for h in range(SIDE):
        out[:, :, h * 256 : h * 256 + 128] = keys[:, :, h * 128 : h * 128 + 128]
        out[:, :, h * 256 + 128 : h * 256 + 256] = values[:, :, h * 128 : h * 128 + 128]


def pair_rows(keys, values):
    shape = keys.shape[:2] + (2 * keys.shape[2],)
    call = small(pair_kernel, jax.ShapeDtypeStruct(shape, keys.dtype), "pair_rows", 1 << 19)
    return call(in_specs=[WHOLE] * 2, out_specs=WHOLE)(keys, values)


def ring(d):
    return [(2 * z + c, 2 * ((z + d) % 8) + c) for z in range(8) for c in range(2)]


def up_z(v):
    return lax.ppermute(v, "ctx", ring(1))


def down_z(v):
    return lax.ppermute(v, "ctx", ring(-1))


def pack_own_kernel(own, queries, out):
    group = queries.shape[2] // (SIDE * HEAD_DIM)
    for h in range(SIDE):
        at = h * 256
        for y in range(SIDE):
            to = SIDE * h + y
            for b in range(2):
                out[to, b * 128 : b * 128 + 64] = own[b, :, at : at + 128]
                out[to, b * 128 + 64 : b * 128 + 128] = own[b, :, at + 128 : at + 256]
                for g in range(group):
                    row = 256 + (b * group + g) * 16
                    column = (h * group + g) * HEAD_DIM
                    out[to, row : row + 16] = queries[
                        b, 16 * y : 16 * y + 16, column : column + HEAD_DIM
                    ]


def pack_own(own, queries):
    rows = 256 + 2 * 16 * queries.shape[2] // (SIDE * HEAD_DIM)
    out = jax.ShapeDtypeStruct((SIDE * SIDE, rows, HEAD_DIM), own.dtype)
    call = small(pack_own_kernel, out, "pack_own", 3 << 20)
    return call(in_specs=[WHOLE] * 2, out_specs=WHOLE)(own, queries)


def pack_listed_kernel(table, block, out):
    for h in range(SIDE):
        at = h * 256
        for y in range(SIDE):
            out[SIDE * h + y, :64] = block[0, :, at : at + 128]
            out[SIDE * h + y, 64:] = block[0, :, at + 128 : at + 256]


def pack_listed(table, everyone):
    rows, width = everyone.shape[1], everyone.shape[2]
    return pl.pallas_call(
        pack_listed_kernel,
        grid_spec=pltpu.PrefetchScalarGridSpec(
            num_scalar_prefetch=1,
            grid=(2,),
            in_specs=[pl.BlockSpec((1, rows, width), lambda i, t: (t[i], 0, 0))],
            out_specs=pl.BlockSpec((16, 128, HEAD_DIM), lambda i, t: (0, i, 0)),
        ),
        out_shape=jax.ShapeDtypeStruct((16, 256, HEAD_DIM), everyone.dtype),
        compiler_params=ordinary(16),
        cost_estimate=pl.CostEstimate(flops=0, bytes_accessed=2 << 20, transcendentals=0),
        name="pack_listed",
    )(table, everyone)


def unpack_kernel(back, out):
    group = out.shape[2] // (SIDE * HEAD_DIM)
    for h in range(SIDE):
        for y in range(SIDE):
            for p in range(2):
                for g in range(group):
                    row = (p * group + g) * 16
                    column = (h * group + g) * HEAD_DIM
                    out[p, 16 * y : 16 * y + 16, column : column + HEAD_DIM] = back[
                        SIDE * h + y, row : row + 16
                    ]


def unpack(back, shape):
    call = small(unpack_kernel, jax.ShapeDtypeStruct(shape, back.dtype), "unpack", 1310720)
    return call(in_specs=[WHOLE], out_specs=WHOLE)(back)


NT = (((1,), (1,)), ((), ()))


def attend_kernel(table, seen, listed, out, kown, vown, klist, vlist):
    p = pl.program_id(0)
    y, usable = table[0], table[1 + p]
    own_at = pl.multiple_of(p * 128, 128)
    for e in range(SIDE * SIDE):
        at = pl.ds(e * 64, 64)
        kown[at, :] = seen[e, pl.ds(own_at, 64), :]
        vown[at, :] = seen[e, pl.ds(own_at + 64, 64), :]
        klist[at, :] = listed[e, pl.ds(own_at, 64), :]
        vlist[at, :] = listed[e, pl.ds(own_at + 64, 64), :]
    scaling = HEAD_DIM ** (-0.5)
    group = out.shape[1] // 32
    rows = 64 * group
    row = lax.rem(lax.broadcasted_iota(jnp.int32, (rows, 256), 0), 64)
    query_pos = lax.div(row, 16) * 64 + 16 * y + lax.rem(row, 16)
    diagonal = lax.broadcasted_iota(jnp.int32, (rows, 256), 1) <= query_pos
    for case in range(SIDE):
        pieces = []
        for g in range(group):
            at = pl.multiple_of(256 + (p * group + g) * 16, 16)
            for e in range(SIDE):
                pieces.append(seen[SIDE * case + e, pl.ds(at, 16), :])
        query = jnp.concatenate(pieces, axis=0)
        before = case * 256
        own = lax.dot_general(
            query, kown[pl.ds(before, 256), :], NT, preferred_element_type=jnp.float32
        )
        own = jnp.where(diagonal, own * scaling, NEGATIVE_LARGE)
        far = lax.dot_general(query, klist[...], NT, preferred_element_type=jnp.float32)
        far = jnp.where(usable > 0, far * scaling, NEGATIVE_LARGE)
        top = jnp.maximum(jnp.max(own, axis=1, keepdims=True), jnp.max(far, axis=1, keepdims=True))
        if case:
            near = lax.dot_general(
                query, kown[pl.ds(0, before), :], NT, preferred_element_type=jnp.float32
            )
            near = near * scaling
            top = jnp.maximum(top, jnp.max(near, axis=1, keepdims=True))
        own = jnp.exp(own - top)
        far = jnp.exp(far - top)
        total = jnp.sum(own, axis=1, keepdims=True) + jnp.sum(far, axis=1, keepdims=True)
        mixed = jnp.dot(
            own.astype(jnp.bfloat16), vown[pl.ds(before, 256), :], preferred_element_type=jnp.float32
        ) + jnp.dot(far.astype(jnp.bfloat16), vlist[...], preferred_element_type=jnp.float32)
        if case:
            near = jnp.exp(near - top)
            total = total + jnp.sum(near, axis=1, keepdims=True)
            mixed = mixed + jnp.dot(
                near.astype(jnp.bfloat16),
                vown[pl.ds(0, before), :],
                preferred_element_type=jnp.float32,
            )
        mixed = (mixed / total).astype(jnp.bfloat16)
        for g in range(group):
            at = pl.multiple_of((p * group + g) * 16, 16)
            for e in range(SIDE):
                start = g * 64 + e * 16
                out[SIDE * case + e, pl.ds(at, 16), :] = mixed[start : start + 16]


def attend(table, seen, listed):
    rows = seen.shape[1] - 256
    out = jax.ShapeDtypeStruct((seen.shape[0], rows, seen.shape[2]), seen.dtype)
    zeros = lambda i, t: (0, 0, 0)
    return pl.pallas_call(
        attend_kernel,
        grid_spec=pltpu.PrefetchScalarGridSpec(
            num_scalar_prefetch=1,
            grid=(2,),
            in_specs=[pl.BlockSpec(seen.shape, zeros), pl.BlockSpec(listed.shape, zeros)],
            out_specs=pl.BlockSpec(out.shape, zeros),
            scratch_shapes=[pltpu.VMEM((1024, HEAD_DIM), jnp.bfloat16)] * 4,
        ),
        out_shape=out,
        compiler_params=ordinary(40),
        cost_estimate=pl.CostEstimate(
            flops=2200000000, bytes_accessed=4 << 20, transcendentals=4300000
        ),
        name="attend",
    )(table, seen, listed)


def listed_rows(block_lists):
    ctx_count = lax.axis_size("ctx")
    blocks_total = 2 * ctx_count
    ctx_index = lax.axis_index("ctx")
    y = lax.rem(lax.axis_index("exp"), SIDE)
    own_blocks = jnp.stack([ctx_index, blocks_total - 1 - ctx_index])
    listed = block_lists[own_blocks]
    usable = (listed != own_blocks).astype(jnp.int32)
    holder = jnp.minimum(listed, blocks_total - 1 - listed)
    row = (2 * holder + (listed >= ctx_count).astype(jnp.int32)).astype(jnp.int32)
    return row, jnp.concatenate([y[None], usable]).astype(jnp.int32)


def trade(v):
    return lax.all_to_all(v, "exp", split_axis=0, concat_axis=0, tiled=True)


def ffn_kernel(places, n_in, refs):
    table, xs, ws = refs[0], refs[1 : 1 + len(places)], refs[1 + len(places) : 7 + len(places)]
    out = refs[n_in]
    rows, gates, downs, act, results, w_sem, x_sem, o_sem = refs[n_in + 1 :]
    width, hidden = gates.shape[1], gates.shape[2]
    loads, stores, at = [], [], 0
    for k, (x, (distance, start)) in enumerate(zip(xs, places)):
        size = x.shape[0]
        span = pl.ds(at, size)
        block = lax.rem(table[0] + distance + 8, 8)
        loads.append(pltpu.make_async_copy(x, rows.at[span, :], x_sem.at[k]))
        stores.append(
            pltpu.make_async_copy(
                results.at[span, :], out.at[block, pl.ds(start, size), :], o_sem.at[k]
            )
        )
        at += size
    targets = [gates.at[0], gates.at[1], gates.at[2], gates.at[3]]
    targets += [downs.at[pl.ds(0, hidden), :], downs.at[pl.ds(hidden, hidden), :]]
    order = (0, 1, 3, 4, 2, 5)
    weights = [pltpu.make_async_copy(ws[w], targets[k], w_sem.at[k]) for k, w in enumerate(order)]
    for copy in loads + weights:
        copy.start()
    for copy in loads:
        copy.wait()
    for half in range(2):
        weights[2 * half].wait()
        gate = jnp.dot(rows[...], gates[2 * half], preferred_element_type=jnp.float32)
        weights[2 * half + 1].wait()
        up = jnp.dot(rows[...], gates[2 * half + 1], preferred_element_type=jnp.float32)
        act[:, half * hidden : (half + 1) * hidden] = (
            gate / (1.0 + jnp.exp(-gate)) * up
        ).astype(jnp.bfloat16)
    weights[4].wait()
    weights[5].wait()
    block = 512

    @pl.loop(0, width // block)
    def _(c):
        columns = pl.ds(pl.multiple_of(c * block, block), block)
        part = jnp.dot(act[...], downs[:, columns], preferred_element_type=jnp.float32)
        results[:, columns] = part.astype(jnp.bfloat16)

    for copy in stores:
        copy.start()
    for copy in stores:
        copy.wait()


def expert_rows(xs, places, weights, table, earlier=None):
    width = xs[0].shape[1]
    hidden = weights[0].shape[1]
    tokens = sum(x.shape[0] for x in xs)
    far = pl.BlockSpec(memory_space=pltpu.HBM)
    operands = [table, *xs, *weights] + ([] if earlier is None else [earlier])
    n_in = len(operands)
    return pl.pallas_call(
        lambda *refs: ffn_kernel(places, n_in, refs),
        in_specs=[TABLE] + [far] * (n_in - 1),
        out_specs=far,
        out_shape=jax.ShapeDtypeStruct((8, 64, width), jnp.bfloat16),
        input_output_aliases={} if earlier is None else {n_in - 1: 0},
        scratch_shapes=[
            pltpu.VMEM((tokens, width), jnp.bfloat16),
            pltpu.VMEM((4, width, hidden), jnp.bfloat16),
            pltpu.VMEM((2 * hidden, width), jnp.bfloat16),
            pltpu.VMEM((tokens, 2 * hidden), jnp.bfloat16),
            pltpu.VMEM((tokens, width), jnp.bfloat16),
            pltpu.SemaphoreType.DMA((6,)),
            pltpu.SemaphoreType.DMA((len(xs),)),
            pltpu.SemaphoreType.DMA((len(xs),)),
        ],
        compiler_params=pltpu.CompilerParams(vmem_limit_bytes=58 * 1024 * 1024),
        cost_estimate=pl.CostEstimate(
            flops=12 * tokens * width * hidden,
            bytes_accessed=12 * width * hidden + 4 * tokens * width,
            transcendentals=2 * tokens * hidden,
        ),
        name="expert_rows",
    )(*operands)


def slot_kernel(hidden, router, ids, out, places):
    experts, tokens, slots = router.shape[0], hidden.shape[0], out.shape[0]
    logits = lax.dot_general(router[...], hidden[...], NT, preferred_element_type=jnp.float32)
    named = ids[...] == lax.broadcasted_iota(jnp.int32, (experts, tokens), 0)
    onehot = jnp.where(named, 1.0, 0.0)
    gate_row = 1.0 / (1.0 + jnp.exp(-jnp.sum(logits * onehot, axis=0, keepdims=True)))
    row = lax.broadcasted_iota(jnp.int32, (tokens, tokens), 0)
    column = lax.broadcasted_iota(jnp.int32, (tokens, tokens), 1)
    upto = jnp.where(row <= column, 1.0, 0.0).astype(jnp.bfloat16)
    counts = jnp.dot(onehot.astype(jnp.bfloat16), upto, preferred_element_type=jnp.float32)
    rank = jnp.sum(counts * onehot, axis=0, keepdims=True) - 1.0
    slot = ids[...] * (slots // experts) + rank.astype(jnp.int32)
    target = lax.broadcasted_iota(jnp.int32, (slots, tokens), 0)
    place = jnp.where(slot == target, 1.0, 0.0).astype(jnp.bfloat16)
    places[...] = place
    gate_score = jnp.sum(jnp.where(row == column, gate_row, 0.0), axis=1, keepdims=True)
    scaled = (hidden[...].astype(jnp.float32) * gate_score).astype(jnp.bfloat16)
    out[...] = jnp.dot(place, scaled, preferred_element_type=jnp.float32).astype(jnp.bfloat16)


def fill_slots(hidden, router, expert_ids, slots):
    tokens, width = hidden.shape
    outs = [
        jax.ShapeDtypeStruct((slots, width), jnp.bfloat16),
        jax.ShapeDtypeStruct((slots, tokens), jnp.bfloat16),
    ]
    call = small(slot_kernel, outs, "fill_slots", 1 << 20)
    return call(in_specs=[WHOLE] * 3, out_specs=[WHOLE] * 2)(hidden, router.T, expert_ids.T)


def route_experts(incoming, places, weights, packed, everyone, row, state, shape):
    model_width = incoming.shape[1]
    exp_count = lax.axis_size("exp")
    half = incoming.shape[0] // 2
    table = lax.div(lax.axis_index("ctx"), 2)[None].astype(jnp.int32)
    below, above = [incoming], [incoming]
    for _ in range(3):
        below.append(up_z(below[-1]))
        above.append(down_z(above[-1]))
    near = expert_rows(
        [incoming, below[1], above[1], below[2], above[2]],
        [(0, 0), (-1, 0), (1, 0), (-2, 0), (2, 0)],
        weights,
        table,
    )
    low, high, near, packed = lax.optimization_barrier((below[3], above[3], near, packed))
    far_low, far_high = up_z(low[:half]), down_z(high[half:])
    listed = trade(pack_listed(row, everyone))
    seen = trade(packed)
    far_low, far_high, listed = lax.optimization_barrier((far_low, far_high, listed))
    partial = expert_rows(
        [low, high, far_low, far_high], [(-3, 0), (3, 0), (4, 0), (4, half)], weights, table, near
    )
    summed_output = lax.psum_scatter(
        partial.reshape(-1, model_width),
        "ctx",
        scatter_dimension=0,
        tiled=True,
        axis_index_groups=RINGS,
    )
    attention = unpack(trade(attend(state, seen, listed)), shape)
    summed_output, attention = lax.optimization_barrier((summed_output, attention))
    returned = trade(summed_output.reshape(exp_count, -1, model_width))
    moe_out = lax.dot_general(
        places,
        returned.reshape(-1, model_width),
        (((0,), (0,)), ((), ())),
        preferred_element_type=jnp.float32,
    ).astype(jnp.bfloat16)
    return attention, moe_out


def shards(
    queries,
    key_states,
    value_state_rows,
    block_lists,
    hidden,
    router,
    expert_ids,
    w_gate,
    w_up,
    w_down,
):
    own = (w_gate[0], w_up[0], w_down[0])
    other = tuple(lax.ppermute(w, "ctx", CORE_SWAP) for w in own)
    experts, width = router.shape[1], router.shape[0]
    capacity = 2 * hidden.shape[0] // experts
    outgoing, places = fill_slots(hidden, router, expert_ids, experts * capacity)
    paired = pair_rows(key_states, value_state_rows)
    everyone = lax.all_gather(paired, "ctx", axis=0, tiled=True)
    incoming = trade(outgoing.reshape(experts, capacity, width)).reshape(-1, width)
    packed = pack_own(paired, queries)
    row, state = listed_rows(block_lists)
    attention, moe_out = route_experts(
        incoming, places, own + other, packed, everyone, row, state, queries.shape
    )
    return (attention, moe_out)


def solution(mesh):
    placed = (
        P(None, ("ctx", "exp"), None),
        P(None, ("ctx", "exp"), None),
        P(None, ("ctx", "exp"), None),
        P(),
        P(("ctx", "exp"), None),
        P(),
        P(("ctx", "exp"), None),
        P("exp", None, "ctx"),
        P("exp", None, "ctx"),
        P("exp", "ctx", None),
    )
    return jax.shard_map(
        shards,
        mesh=mesh,
        in_specs=placed,
        out_specs=(P(None, ("ctx", "exp"), None), P(("ctx", "exp"), None)),
        check_vma=False,
    )
```

```python
import functools

import jax
import jax.numpy as jnp
from jax import lax
from jax.experimental import pallas as pl
from jax.experimental.pallas import tpu as pltpu
from jax.sharding import PartitionSpec as P

HEAD_DIM = 128
NEGATIVE_LARGE = -1e30
SIDE = 4
RINGS = [[2 * z + c for z in range(8)] for c in range(2)]
CORE_SWAP = [(i, i ^ 1) for i in range(16)]


def ordinary(vmem=48):
    return pltpu.CompilerParams(
        dimension_semantics=("arbitrary",), vmem_limit_bytes=vmem * 1024 * 1024
    )


WHOLE = pl.BlockSpec(memory_space=pltpu.VMEM)
TABLE = pl.BlockSpec(memory_space=pltpu.SMEM)


def small(kernel, outs, name, moved, scratch=()):
    return functools.partial(
        pl.pallas_call,
        kernel,
        out_shape=outs,
        scratch_shapes=scratch,
        compiler_params=pltpu.CompilerParams(vmem_limit_bytes=16 * 1024 * 1024),
        cost_estimate=pl.CostEstimate(flops=0, bytes_accessed=moved, transcendentals=0),
        name=name,
    )


def pair_kernel(keys, values, out):
    for h in range(SIDE):
        out[:, :, h * 256 : h * 256 + 128] = keys[:, :, h * 128 : h * 128 + 128]
        out[:, :, h * 256 + 128 : h * 256 + 256] = values[:, :, h * 128 : h * 128 + 128]


def pair_rows(keys, values):
    shape = keys.shape[:2] + (2 * keys.shape[2],)
    call = small(pair_kernel, jax.ShapeDtypeStruct(shape, keys.dtype), "pair_rows", 1 << 19)
    return call(in_specs=[WHOLE] * 2, out_specs=WHOLE)(keys, values)


def ring(d):
    return [(2 * z + c, 2 * ((z + d) % 8) + c) for z in range(8) for c in range(2)]


def up_z(v):
    return lax.ppermute(v, "ctx", ring(1))


def down_z(v):
    return lax.ppermute(v, "ctx", ring(-1))


def pack_own_kernel(own, queries, out):
    group = queries.shape[2] // (SIDE * HEAD_DIM)
    for h in range(SIDE):
        at = h * 256
        for y in range(SIDE):
            to = SIDE * h + y
            for b in range(2):
                out[to, b * 128 : b * 128 + 64] = own[b, :, at : at + 128]
                out[to, b * 128 + 64 : b * 128 + 128] = own[b, :, at + 128 : at + 256]
                for g in range(group):
                    row = 256 + (b * group + g) * 16
                    column = (h * group + g) * HEAD_DIM
                    out[to, row : row + 16] = queries[
                        b, 16 * y : 16 * y + 16, column : column + HEAD_DIM
                    ]


def pack_own(own, queries):
    rows = 256 + 2 * 16 * queries.shape[2] // (SIDE * HEAD_DIM)
    out = jax.ShapeDtypeStruct((SIDE * SIDE, rows, HEAD_DIM), own.dtype)
    call = small(pack_own_kernel, out, "pack_own", 3 << 20)
    return call(in_specs=[WHOLE] * 2, out_specs=WHOLE)(own, queries)


def pack_listed_kernel(table, block, out):
    for h in range(SIDE):
        at = h * 256
        for y in range(SIDE):
            out[SIDE * h + y, :64] = block[0, :, at : at + 128]
            out[SIDE * h + y, 64:] = block[0, :, at + 128 : at + 256]


def pack_listed(table, everyone):
    rows, width = everyone.shape[1], everyone.shape[2]
    return pl.pallas_call(
        pack_listed_kernel,
        grid_spec=pltpu.PrefetchScalarGridSpec(
            num_scalar_prefetch=1,
            grid=(2,),
            in_specs=[pl.BlockSpec((1, rows, width), lambda i, t: (t[i], 0, 0))],
            out_specs=pl.BlockSpec((16, 128, HEAD_DIM), lambda i, t: (0, i, 0)),
        ),
        out_shape=jax.ShapeDtypeStruct((16, 256, HEAD_DIM), everyone.dtype),
        compiler_params=ordinary(16),
        cost_estimate=pl.CostEstimate(flops=0, bytes_accessed=2 << 20, transcendentals=0),
        name="pack_listed",
    )(table, everyone)


def unpack_kernel(back, out):
    group = out.shape[2] // (SIDE * HEAD_DIM)
    for h in range(SIDE):
        for y in range(SIDE):
            for p in range(2):
                for g in range(group):
                    row = (p * group + g) * 16
                    column = (h * group + g) * HEAD_DIM
                    out[p, 16 * y : 16 * y + 16, column : column + HEAD_DIM] = back[
                        SIDE * h + y, row : row + 16
                    ]


def unpack(back, shape):
    call = small(unpack_kernel, jax.ShapeDtypeStruct(shape, back.dtype), "unpack", 1310720)
    return call(in_specs=[WHOLE], out_specs=WHOLE)(back)


NT = (((1,), (1,)), ((), ()))


def attend_kernel(table, seen, listed, out, kown, vown, klist, vlist):
    p = pl.program_id(0)
    y, usable = table[0], table[1 + p]
    own_at = pl.multiple_of(p * 128, 128)
    for e in range(SIDE * SIDE):
        at = pl.ds(e * 64, 64)
        kown[at, :] = seen[e, pl.ds(own_at, 64), :]
        vown[at, :] = seen[e, pl.ds(own_at + 64, 64), :]
        klist[at, :] = listed[e, pl.ds(own_at, 64), :]
        vlist[at, :] = listed[e, pl.ds(own_at + 64, 64), :]
    scaling = HEAD_DIM ** (-0.5)
    group = out.shape[1] // 32
    rows = 64 * group
    row = lax.rem(lax.broadcasted_iota(jnp.int32, (rows, 256), 0), 64)
    query_pos = lax.div(row, 16) * 64 + 16 * y + lax.rem(row, 16)
    diagonal = lax.broadcasted_iota(jnp.int32, (rows, 256), 1) <= query_pos
    for case in range(SIDE):
        pieces = []
        for g in range(group):
            at = pl.multiple_of(256 + (p * group + g) * 16, 16)
            for e in range(SIDE):
                pieces.append(seen[SIDE * case + e, pl.ds(at, 16), :])
        query = jnp.concatenate(pieces, axis=0)
        before = case * 256
        own = lax.dot_general(
            query, kown[pl.ds(before, 256), :], NT, preferred_element_type=jnp.float32
        )
        own = jnp.where(diagonal, own * scaling, NEGATIVE_LARGE)
        far = lax.dot_general(query, klist[...], NT, preferred_element_type=jnp.float32)
        far = jnp.where(usable > 0, far * scaling, NEGATIVE_LARGE)
        top = jnp.maximum(jnp.max(own, axis=1, keepdims=True), jnp.max(far, axis=1, keepdims=True))
        if case:
            near = lax.dot_general(
                query, kown[pl.ds(0, before), :], NT, preferred_element_type=jnp.float32
            )
            near = near * scaling
            top = jnp.maximum(top, jnp.max(near, axis=1, keepdims=True))
        own = jnp.exp(own - top)
        far = jnp.exp(far - top)
        total = jnp.sum(own, axis=1, keepdims=True) + jnp.sum(far, axis=1, keepdims=True)
        mixed = jnp.dot(
            own.astype(jnp.bfloat16), vown[pl.ds(before, 256), :], preferred_element_type=jnp.float32
        ) + jnp.dot(far.astype(jnp.bfloat16), vlist[...], preferred_element_type=jnp.float32)
        if case:
            near = jnp.exp(near - top)
            total = total + jnp.sum(near, axis=1, keepdims=True)
            mixed = mixed + jnp.dot(
                near.astype(jnp.bfloat16),
                vown[pl.ds(0, before), :],
                preferred_element_type=jnp.float32,
            )
        mixed = (mixed / total).astype(jnp.bfloat16)
        for g in range(group):
            at = pl.multiple_of((p * group + g) * 16, 16)
            for e in range(SIDE):
                start = g * 64 + e * 16
                out[SIDE * case + e, pl.ds(at, 16), :] = mixed[start : start + 16]


def attend(table, seen, listed):
    rows = seen.shape[1] - 256
    out = jax.ShapeDtypeStruct((seen.shape[0], rows, seen.shape[2]), seen.dtype)
    zeros = lambda i, t: (0, 0, 0)
    return pl.pallas_call(
        attend_kernel,
        grid_spec=pltpu.PrefetchScalarGridSpec(
            num_scalar_prefetch=1,
            grid=(2,),
            in_specs=[pl.BlockSpec(seen.shape, zeros), pl.BlockSpec(listed.shape, zeros)],
            out_specs=pl.BlockSpec(out.shape, zeros),
            scratch_shapes=[pltpu.VMEM((1024, HEAD_DIM), jnp.bfloat16)] * 4,
        ),
        out_shape=out,
        compiler_params=ordinary(40),
        cost_estimate=pl.CostEstimate(
            flops=2200000000, bytes_accessed=4 << 20, transcendentals=4300000
        ),
        name="attend",
    )(table, seen, listed)


def listed_rows(block_lists):
    ctx_count = lax.axis_size("ctx")
    blocks_total = 2 * ctx_count
    ctx_index = lax.axis_index("ctx")
    y = lax.rem(lax.axis_index("exp"), SIDE)
    own_blocks = jnp.stack([ctx_index, blocks_total - 1 - ctx_index])
    listed = block_lists[own_blocks]
    usable = (listed != own_blocks).astype(jnp.int32)
    holder = jnp.minimum(listed, blocks_total - 1 - listed)
    row = (2 * holder + (listed >= ctx_count).astype(jnp.int32)).astype(jnp.int32)
    return row, jnp.concatenate([y[None], usable]).astype(jnp.int32)


def trade(v):
    return lax.all_to_all(v, "exp", split_axis=0, concat_axis=0, tiled=True)


def ffn_kernel(places, n_in, refs):
    count = len(places)
    table, xs, ws = refs[0], refs[1 : 1 + count], refs[1 + count : 7 + count]
    out = refs[n_in]
    rows, gates, downs, act, results, w_sem, x_sem, o_sem = refs[n_in + 1 :]
    width, hidden = gates.shape[1], gates.shape[2]
    loads, stores, at = [], [], 0
    for k, x in enumerate(xs):
        loads.append(
            pltpu.make_async_copy(x, rows.at[pl.ds(at, x.shape[0]), :], x_sem.at[k])
        )
        for size, relative, number, start in places[k]:
            block = lax.rem(table[0] + number + 8, 8) if relative else number
            stores.append(
                pltpu.make_async_copy(
                    results.at[pl.ds(at, size), :],
                    out.at[block, pl.ds(start, size), :],
                    o_sem.at[len(stores)],
                )
            )
            at += size
    targets = [gates.at[0], gates.at[1], gates.at[2], gates.at[3]]
    targets += [downs.at[pl.ds(0, hidden), :], downs.at[pl.ds(hidden, hidden), :]]
    order = (0, 1, 3, 4, 2, 5)
    weights = [pltpu.make_async_copy(ws[w], targets[k], w_sem.at[k]) for k, w in enumerate(order)]
    for copy in loads + weights:
        copy.start()
    for copy in loads:
        copy.wait()
    for half in range(2):
        weights[2 * half].wait()
        gate = jnp.dot(rows[...], gates[2 * half], preferred_element_type=jnp.float32)
        weights[2 * half + 1].wait()
        up = jnp.dot(rows[...], gates[2 * half + 1], preferred_element_type=jnp.float32)
        act[:, half * hidden : (half + 1) * hidden] = (
            gate / (1.0 + jnp.exp(-gate)) * up
        ).astype(jnp.bfloat16)
    weights[4].wait()
    weights[5].wait()
    block = 512

    @pl.loop(0, width // block)
    def _(c):
        columns = pl.ds(pl.multiple_of(c * block, block), block)
        part = jnp.dot(act[...], downs[:, columns], preferred_element_type=jnp.float32)
        results[:, columns] = part.astype(jnp.bfloat16)

    for copy in stores:
        copy.start()
    for copy in stores:
        copy.wait()


def expert_rows(xs, places, weights, table, earlier=None):
    width = xs[0].shape[1]
    hidden = weights[0].shape[1]
    tokens = sum(x.shape[0] for x in xs)
    far = pl.BlockSpec(memory_space=pltpu.HBM)
    operands = [table, *xs, *weights] + ([] if earlier is None else [earlier])
    n_in = len(operands)
    return pl.pallas_call(
        lambda *refs: ffn_kernel(places, n_in, refs),
        in_specs=[TABLE] + [far] * (n_in - 1),
        out_specs=far,
        out_shape=jax.ShapeDtypeStruct((8, 64, width), jnp.bfloat16),
        input_output_aliases={} if earlier is None else {n_in - 1: 0},
        scratch_shapes=[
            pltpu.VMEM((tokens, width), jnp.bfloat16),
            pltpu.VMEM((4, width, hidden), jnp.bfloat16),
            pltpu.VMEM((2 * hidden, width), jnp.bfloat16),
            pltpu.VMEM((tokens, 2 * hidden), jnp.bfloat16),
            pltpu.VMEM((tokens, width), jnp.bfloat16),
            pltpu.SemaphoreType.DMA((6,)),
            pltpu.SemaphoreType.DMA((len(xs),)),
            pltpu.SemaphoreType.DMA((sum(len(p) for p in places),)),
        ],
        compiler_params=pltpu.CompilerParams(vmem_limit_bytes=58 * 1024 * 1024),
        cost_estimate=pl.CostEstimate(
            flops=12 * tokens * width * hidden,
            bytes_accessed=12 * width * hidden + 4 * tokens * width,
            transcendentals=2 * tokens * hidden,
        ),
        name="expert_rows",
    )(*operands)


def slot_kernel(hidden, router, ids, out, places):
    experts, tokens, slots = router.shape[0], hidden.shape[0], out.shape[0]
    logits = lax.dot_general(router[...], hidden[...], NT, preferred_element_type=jnp.float32)
    named = ids[...] == lax.broadcasted_iota(jnp.int32, (experts, tokens), 0)
    onehot = jnp.where(named, 1.0, 0.0)
    gate_row = 1.0 / (1.0 + jnp.exp(-jnp.sum(logits * onehot, axis=0, keepdims=True)))
    row = lax.broadcasted_iota(jnp.int32, (tokens, tokens), 0)
    column = lax.broadcasted_iota(jnp.int32, (tokens, tokens), 1)
    upto = jnp.where(row <= column, 1.0, 0.0).astype(jnp.bfloat16)
    counts = jnp.dot(onehot.astype(jnp.bfloat16), upto, preferred_element_type=jnp.float32)
    rank = jnp.sum(counts * onehot, axis=0, keepdims=True) - 1.0
    slot = ids[...] * (slots // experts) + rank.astype(jnp.int32)
    target = lax.broadcasted_iota(jnp.int32, (slots, tokens), 0)
    place = jnp.where(slot == target, 1.0, 0.0).astype(jnp.bfloat16)
    places[...] = place
    gate_score = jnp.sum(jnp.where(row == column, gate_row, 0.0), axis=1, keepdims=True)
    scaled = (hidden[...].astype(jnp.float32) * gate_score).astype(jnp.bfloat16)
    out[...] = jnp.dot(place, scaled, preferred_element_type=jnp.float32).astype(jnp.bfloat16)


def fill_slots(hidden, router, expert_ids, slots):
    tokens, width = hidden.shape
    outs = [
        jax.ShapeDtypeStruct((slots, width), jnp.bfloat16),
        jax.ShapeDtypeStruct((slots, tokens), jnp.bfloat16),
    ]
    call = small(slot_kernel, outs, "fill_slots", 1 << 20)
    return call(in_specs=[WHOLE] * 3, out_specs=[WHOLE] * 2)(hidden, router.T, expert_ids.T)


def route_experts(incoming, places, weights, packed, everyone, row, state, shape):
    model_width = incoming.shape[1]
    exp_count = lax.axis_size("exp")
    part = incoming.shape[0] // 2
    half = part // 2
    table = lax.div(lax.axis_index("ctx"), 2)[None].astype(jnp.int32)
    rows = lax.all_gather(
        incoming[part:], "ctx", axis=0, tiled=True, axis_index_groups=RINGS
    )
    kept = incoming[:part]
    below, above = [kept], [kept]
    for _ in range(3):
        below.append(up_z(below[-1]))
        above.append(down_z(above[-1]))
    near = expert_rows(
        [kept, below[1], above[1], below[2], above[2]],
        [[(part, True, d, 0)] for d in (0, -1, 1, -2, 2)],
        weights,
        table,
    )
    far_low, far_high = up_z(below[3][:half]), down_z(above[3][half:])
    seen = trade(packed)
    near, far_low, far_high, rows, seen = lax.optimization_barrier(
        (near, far_low, far_high, rows, seen)
    )
    partial = expert_rows(
        [below[3], above[3], far_low, far_high, rows],
        [
            [(part, True, -3, 0)],
            [(part, True, 3, 0)],
            [(half, True, 4, 0)],
            [(half, True, 4, half)],
            [(part, False, j, part) for j in range(8)],
        ],
        weights,
        table,
        near,
    )
    everyone, partial = lax.optimization_barrier((everyone, partial))
    listed = trade(pack_listed(row, everyone))
    summed_output = lax.psum_scatter(
        partial.reshape(-1, model_width),
        "ctx",
        scatter_dimension=0,
        tiled=True,
        axis_index_groups=RINGS,
    )
    attention = unpack(trade(attend(state, seen, listed)), shape)
    summed_output, attention = lax.optimization_barrier((summed_output, attention))
    returned = trade(summed_output.reshape(exp_count, -1, model_width))
    moe_out = lax.dot_general(
        places,
        returned.reshape(-1, model_width),
        (((0,), (0,)), ((), ())),
        preferred_element_type=jnp.float32,
    ).astype(jnp.bfloat16)
    return attention, moe_out


def shards(
    queries,
    key_states,
    value_state_rows,
    block_lists,
    hidden,
    router,
    expert_ids,
    w_gate,
    w_up,
    w_down,
):
    own = (w_gate[0], w_up[0], w_down[0])
    other = tuple(lax.ppermute(w, "ctx", CORE_SWAP) for w in own)
    experts, width = router.shape[1], router.shape[0]
    capacity = 2 * hidden.shape[0] // experts
    outgoing, places = fill_slots(hidden, router, expert_ids, experts * capacity)
    paired = pair_rows(key_states, value_state_rows)
    everyone = lax.all_gather(paired, "ctx", axis=0, tiled=True)
    incoming = trade(outgoing.reshape(experts, capacity, width)).reshape(-1, width)
    packed = pack_own(paired, queries)
    row, state = listed_rows(block_lists)
    attention, moe_out = route_experts(
        incoming, places, own + other, packed, everyone, row, state, queries.shape
    )
    return (attention, moe_out)


def solution(mesh):
    placed = (
        P(None, ("ctx", "exp"), None),
        P(None, ("ctx", "exp"), None),
        P(None, ("ctx", "exp"), None),
        P(),
        P(("ctx", "exp"), None),
        P(),
        P(("ctx", "exp"), None),
        P("exp", None, "ctx"),
        P("exp", None, "ctx"),
        P("exp", "ctx", None),
    )
    return jax.shard_map(
        shards,
        mesh=mesh,
        in_specs=placed,
        out_specs=(P(None, ("ctx", "exp"), None), P(("ctx", "exp"), None)),
        check_vma=False,
    )
```

```python
import functools

import jax
import jax.numpy as jnp
from jax import lax
from jax.experimental import pallas as pl
from jax.experimental.pallas import tpu as pltpu
from jax.sharding import PartitionSpec as P

HEAD_DIM = 128
NEGATIVE_LARGE = -1e30
SIDE = 4
RINGS = [[2 * z + c for z in range(8)] for c in range(2)]
CORE_SWAP = [(i, i ^ 1) for i in range(16)]


def ordinary(vmem=48):
    return pltpu.CompilerParams(
        dimension_semantics=("arbitrary",), vmem_limit_bytes=vmem * 1024 * 1024
    )


WHOLE = pl.BlockSpec(memory_space=pltpu.VMEM)
TABLE = pl.BlockSpec(memory_space=pltpu.SMEM)


def small(kernel, outs, name, moved, scratch=()):
    return functools.partial(
        pl.pallas_call,
        kernel,
        out_shape=outs,
        scratch_shapes=scratch,
        compiler_params=pltpu.CompilerParams(vmem_limit_bytes=16 * 1024 * 1024),
        cost_estimate=pl.CostEstimate(flops=0, bytes_accessed=moved, transcendentals=0),
        name=name,
    )


def pair_kernel(keys, values, out):
    for h in range(SIDE):
        out[:, :, h * 256 : h * 256 + 128] = keys[:, :, h * 128 : h * 128 + 128]
        out[:, :, h * 256 + 128 : h * 256 + 256] = values[:, :, h * 128 : h * 128 + 128]


def pair_rows(keys, values):
    shape = keys.shape[:2] + (2 * keys.shape[2],)
    call = small(pair_kernel, jax.ShapeDtypeStruct(shape, keys.dtype), "pair_rows", 1 << 19)
    return call(in_specs=[WHOLE] * 2, out_specs=WHOLE)(keys, values)


def ring(d):
    return [(2 * z + c, 2 * ((z + d) % 8) + c) for z in range(8) for c in range(2)]


def up_z(v):
    return lax.ppermute(v, "ctx", ring(1))


def down_z(v):
    return lax.ppermute(v, "ctx", ring(-1))


def choose_kernel(table, *refs):
    own, b1, b2, b3, far_low, far_high, a3, a2, a1, mine, theirs, held = refs
    for k, block in ((0, own), (1, b1), (2, b2), (3, b3), (5, a3), (6, a2), (7, a1)):
        held[2 * k] = block[0]
        held[2 * k + 1] = block[1]
    held[8] = far_low[0]
    held[9] = far_high[0]
    for i in range(2):
        mine[i] = held[table[i]]
        theirs[i] = held[table[2 + i]]


def choose_blocks(below, above, table):
    paired = below[0]
    far_low, far_high = up_z(below[3][:1]), down_z(above[3][1:])
    out = jax.ShapeDtypeStruct(paired.shape, paired.dtype)
    held = pltpu.VMEM((16,) + paired.shape[1:], paired.dtype)
    call = small(choose_kernel, [out, out], "choose_blocks", 3 << 20, [held])
    return call(in_specs=[TABLE] + [WHOLE] * 9, out_specs=[WHOLE] * 2)(
        table, paired, *below[1:], far_low, far_high, above[3], above[2], above[1]
    )


def pack_own_kernel(own, queries, out):
    group = queries.shape[2] // (SIDE * HEAD_DIM)
    for h in range(SIDE):
        at = h * 256
        for y in range(SIDE):
            to = SIDE * h + y
            for b in range(2):
                out[to, b * 128 : b * 128 + 64] = own[b, :, at : at + 128]
                out[to, b * 128 + 64 : b * 128 + 128] = own[b, :, at + 128 : at + 256]
                for g in range(group):
                    row = 256 + (b * group + g) * 16
                    column = (h * group + g) * HEAD_DIM
                    out[to, row : row + 16] = queries[
                        b, 16 * y : 16 * y + 16, column : column + HEAD_DIM
                    ]


def pack_own(own, queries):
    rows = 256 + 2 * 16 * queries.shape[2] // (SIDE * HEAD_DIM)
    out = jax.ShapeDtypeStruct((SIDE * SIDE, rows, HEAD_DIM), own.dtype)
    call = small(pack_own_kernel, out, "pack_own", 3 << 20)
    return call(in_specs=[WHOLE] * 2, out_specs=WHOLE)(own, queries)


def pack_listed_kernel(table, mine, swapped, out):
    for h in range(SIDE):
        at = h * 256
        for b in range(2):
            piece = jnp.where(
                table[b] > 0, mine[b, :, at : at + 256], swapped[b, :, at : at + 256]
            )
            for y in range(SIDE):
                out[SIDE * h + y, b * 128 : b * 128 + 64] = piece[:, :HEAD_DIM]
                out[SIDE * h + y, b * 128 + 64 : b * 128 + 128] = piece[:, HEAD_DIM:]


def pack_listed(table, mine, swapped):
    out = jax.ShapeDtypeStruct((SIDE * SIDE, 256, HEAD_DIM), mine.dtype)
    call = small(pack_listed_kernel, out, "pack_listed", 3 << 20)
    return call(in_specs=[TABLE] + [WHOLE] * 2, out_specs=WHOLE)(table, mine, swapped)


def unpack_kernel(back, out):
    group = out.shape[2] // (SIDE * HEAD_DIM)
    for h in range(SIDE):
        for y in range(SIDE):
            for p in range(2):
                for g in range(group):
                    row = (p * group + g) * 16
                    column = (h * group + g) * HEAD_DIM
                    out[p, 16 * y : 16 * y + 16, column : column + HEAD_DIM] = back[
                        SIDE * h + y, row : row + 16
                    ]


def unpack(back, shape):
    call = small(unpack_kernel, jax.ShapeDtypeStruct(shape, back.dtype), "unpack", 1310720)
    return call(in_specs=[WHOLE], out_specs=WHOLE)(back)


NT = (((1,), (1,)), ((), ()))


def attend_kernel(table, seen, listed, out, kown, vown, klist, vlist):
    p = pl.program_id(0)
    y, usable = table[0], table[1 + p]
    own_at = pl.multiple_of(p * 128, 128)
    for e in range(SIDE * SIDE):
        at = pl.ds(e * 64, 64)
        kown[at, :] = seen[e, pl.ds(own_at, 64), :]
        vown[at, :] = seen[e, pl.ds(own_at + 64, 64), :]
        klist[at, :] = listed[e, pl.ds(own_at, 64), :]
        vlist[at, :] = listed[e, pl.ds(own_at + 64, 64), :]
    scaling = HEAD_DIM ** (-0.5)
    group = out.shape[1] // 32
    rows = 64 * group
    row = lax.rem(lax.broadcasted_iota(jnp.int32, (rows, 256), 0), 64)
    query_pos = lax.div(row, 16) * 64 + 16 * y + lax.rem(row, 16)
    diagonal = lax.broadcasted_iota(jnp.int32, (rows, 256), 1) <= query_pos
    for case in range(SIDE):
        pieces = []
        for g in range(group):
            at = pl.multiple_of(256 + (p * group + g) * 16, 16)
            for e in range(SIDE):
                pieces.append(seen[SIDE * case + e, pl.ds(at, 16), :])
        query = jnp.concatenate(pieces, axis=0)
        before = case * 256
        own = lax.dot_general(
            query, kown[pl.ds(before, 256), :], NT, preferred_element_type=jnp.float32
        )
        own = jnp.where(diagonal, own * scaling, NEGATIVE_LARGE)
        far = lax.dot_general(query, klist[...], NT, preferred_element_type=jnp.float32)
        far = jnp.where(usable > 0, far * scaling, NEGATIVE_LARGE)
        top = jnp.maximum(jnp.max(own, axis=1, keepdims=True), jnp.max(far, axis=1, keepdims=True))
        if case:
            near = lax.dot_general(
                query, kown[pl.ds(0, before), :], NT, preferred_element_type=jnp.float32
            )
            near = near * scaling
            top = jnp.maximum(top, jnp.max(near, axis=1, keepdims=True))
        own = jnp.exp(own - top)
        far = jnp.exp(far - top)
        total = jnp.sum(own, axis=1, keepdims=True) + jnp.sum(far, axis=1, keepdims=True)
        mixed = jnp.dot(
            own.astype(jnp.bfloat16), vown[pl.ds(before, 256), :], preferred_element_type=jnp.float32
        ) + jnp.dot(far.astype(jnp.bfloat16), vlist[...], preferred_element_type=jnp.float32)
        if case:
            near = jnp.exp(near - top)
            total = total + jnp.sum(near, axis=1, keepdims=True)
            mixed = mixed + jnp.dot(
                near.astype(jnp.bfloat16),
                vown[pl.ds(0, before), :],
                preferred_element_type=jnp.float32,
            )
        mixed = (mixed / total).astype(jnp.bfloat16)
        for g in range(group):
            at = pl.multiple_of((p * group + g) * 16, 16)
            for e in range(SIDE):
                start = g * 64 + e * 16
                out[SIDE * case + e, pl.ds(at, 16), :] = mixed[start : start + 16]


def attend(table, seen, listed):
    rows = seen.shape[1] - 256
    out = jax.ShapeDtypeStruct((seen.shape[0], rows, seen.shape[2]), seen.dtype)
    zeros = lambda i, t: (0, 0, 0)
    return pl.pallas_call(
        attend_kernel,
        grid_spec=pltpu.PrefetchScalarGridSpec(
            num_scalar_prefetch=1,
            grid=(2,),
            in_specs=[pl.BlockSpec(seen.shape, zeros), pl.BlockSpec(listed.shape, zeros)],
            out_specs=pl.BlockSpec(out.shape, zeros),
            scratch_shapes=[pltpu.VMEM((1024, HEAD_DIM), jnp.bfloat16)] * 4,
        ),
        out_shape=out,
        compiler_params=ordinary(40),
        cost_estimate=pl.CostEstimate(
            flops=2200000000, bytes_accessed=4 << 20, transcendentals=4300000
        ),
        name="attend",
    )(table, seen, listed)


def exchange_rows(below, above, block_lists):
    ctx_count = lax.axis_size("ctx")
    blocks_total = 2 * ctx_count
    ctx_index = lax.axis_index("ctx")
    exp_index = lax.axis_index("exp")
    y = lax.rem(exp_index, SIDE)
    z, core = lax.div(ctx_index, 2), lax.rem(ctx_index, 2)
    other = ctx_index + 1 - 2 * core
    own_blocks = jnp.stack(
        [ctx_index, blocks_total - 1 - ctx_index, other, blocks_total - 1 - other]
    )
    listed = block_lists[own_blocks]
    usable = (listed != own_blocks).astype(jnp.int32)
    holder = jnp.minimum(listed, blocks_total - 1 - listed)
    distance = lax.rem(z + 8 - lax.div(holder, 2), 8)
    chosen = (2 * distance + (listed >= ctx_count).astype(jnp.int32)).astype(jnp.int32)
    local = (lax.rem(holder, 2) == core).astype(jnp.int32)

    mine, theirs = choose_blocks(below, above, chosen)
    swapped = lax.ppermute(theirs, "ctx", CORE_SWAP)
    packed = pack_listed(local[:2], mine, swapped)
    return packed, jnp.concatenate([y[None], usable[:2]]).astype(jnp.int32)


def trade(v):
    return lax.all_to_all(v, "exp", split_axis=0, concat_axis=0, tiled=True)


def ffn_kernel(counts, refs):
    xs, ws, outs = refs[:counts], refs[counts : counts + 6], refs[counts + 6 : 2 * counts + 6]
    rows, gates, downs, results, act, w_sem, x_sem, o_sem = refs[2 * counts + 6 :]
    width, hidden = gates.shape[1], gates.shape[2] // 2
    step = rows.shape[1]
    parts = []
    for x, out in zip(xs, outs):
        for at in range(0, x.shape[0], step):
            parts.append((x, out, at, min(step, x.shape[0] - at)))
    loads = [
        pltpu.make_async_copy(
            x.at[pl.ds(at, n), :], rows.at[k, pl.ds(0, n), :], x_sem.at[k]
        )
        for k, (x, _, at, n) in enumerate(parts)
    ]
    stores = [
        pltpu.make_async_copy(
            results.at[k, pl.ds(0, n), :], out.at[pl.ds(at, n), :], o_sem.at[k]
        )
        for k, (_, out, at, n) in enumerate(parts)
    ]
    targets = [gates.at[h, :, pl.ds(c * hidden, hidden)] for h in range(2) for c in range(2)]
    targets += [downs.at[pl.ds(0, hidden), :], downs.at[pl.ds(hidden, hidden), :]]
    order = (0, 1, 3, 4, 2, 5)
    weights = [pltpu.make_async_copy(ws[w], targets[k], w_sem.at[k]) for k, w in enumerate(order)]
    loads[0].start()
    for copy in weights:
        copy.start()
    for copy in loads[1:]:
        copy.start()
    block = 1024
    for k, (x, out, at, n) in enumerate(parts):
        loads[k].wait()
        for half in range(2):
            if k == 0:
                weights[2 * half].wait()
                weights[2 * half + 1].wait()
            both = jnp.dot(rows[k, :n], gates[half], preferred_element_type=jnp.float32)
            gate, up = both[:, :hidden], both[:, hidden:]
            act[:n, half * hidden : (half + 1) * hidden] = (
                gate / (1.0 + jnp.exp(-gate)) * up
            ).astype(jnp.bfloat16)
        if k == 0:
            weights[4].wait()
            weights[5].wait()

        @pl.loop(0, width // block)
        def _(c, k=k, n=n):
            columns = pl.ds(pl.multiple_of(c * block, block), block)
            part = jnp.dot(act[:n], downs[:, columns], preferred_element_type=jnp.float32)
            results[k, :n, columns] = part.astype(jnp.bfloat16)

        stores[k].start()
    for copy in stores:
        copy.wait()


def expert_rows(xs, weights, step=256):
    width = xs[0].shape[1]
    hidden = weights[0].shape[1]
    tokens = sum(x.shape[0] for x in xs)
    step = min(step, max(x.shape[0] for x in xs))
    parts = sum(-(-x.shape[0] // step) for x in xs)
    far = pl.BlockSpec(memory_space=pltpu.HBM)
    return pl.pallas_call(
        lambda *refs: ffn_kernel(len(xs), refs),
        in_specs=[far] * (len(xs) + 6),
        out_specs=[far] * len(xs),
        out_shape=[jax.ShapeDtypeStruct(x.shape, jnp.bfloat16) for x in xs],
        scratch_shapes=[
            pltpu.VMEM((parts, step, width), jnp.bfloat16),
            pltpu.VMEM((2, width, 2 * hidden), jnp.bfloat16),
            pltpu.VMEM((2 * hidden, width), jnp.bfloat16),
            pltpu.VMEM((parts, step, width), jnp.bfloat16),
            pltpu.VMEM((step, 2 * hidden), jnp.bfloat16),
            pltpu.SemaphoreType.DMA((6,)),
            pltpu.SemaphoreType.DMA((parts,)),
            pltpu.SemaphoreType.DMA((parts,)),
        ],
        compiler_params=pltpu.CompilerParams(vmem_limit_bytes=60 * 1024 * 1024),
        cost_estimate=pl.CostEstimate(
            flops=12 * tokens * width * hidden,
            bytes_accessed=12 * width * hidden + 4 * tokens * width,
            transcendentals=2 * tokens * hidden,
        ),
        name="expert_rows",
    )(*xs, *weights)


def slot_kernel(hidden, router, ids, out, places):
    experts, tokens, slots = router.shape[0], hidden.shape[0], out.shape[0]
    logits = lax.dot_general(router[...], hidden[...], NT, preferred_element_type=jnp.float32)
    named = ids[...] == lax.broadcasted_iota(jnp.int32, (experts, tokens), 0)
    onehot = jnp.where(named, 1.0, 0.0)
    gate_row = 1.0 / (1.0 + jnp.exp(-jnp.sum(logits * onehot, axis=0, keepdims=True)))
    row = lax.broadcasted_iota(jnp.int32, (tokens, tokens), 0)
    column = lax.broadcasted_iota(jnp.int32, (tokens, tokens), 1)
    upto = jnp.where(row <= column, 1.0, 0.0).astype(jnp.bfloat16)
    counts = jnp.dot(onehot.astype(jnp.bfloat16), upto, preferred_element_type=jnp.float32)
    rank = jnp.sum(counts * onehot, axis=0, keepdims=True) - 1.0
    slot = ids[...] * (slots // experts) + rank.astype(jnp.int32)
    target = lax.broadcasted_iota(jnp.int32, (slots, tokens), 0)
    place = jnp.where(slot == target, 1.0, 0.0).astype(jnp.bfloat16)
    places[...] = place
    gate_score = jnp.sum(jnp.where(row == column, gate_row, 0.0), axis=1, keepdims=True)
    scaled = (hidden[...].astype(jnp.float32) * gate_score).astype(jnp.bfloat16)
    out[...] = jnp.dot(place, scaled, preferred_element_type=jnp.float32).astype(jnp.bfloat16)


def fill_slots(hidden, router, expert_ids, slots):
    tokens, width = hidden.shape
    outs = [
        jax.ShapeDtypeStruct((slots, width), jnp.bfloat16),
        jax.ShapeDtypeStruct((slots, tokens), jnp.bfloat16),
    ]
    call = small(slot_kernel, outs, "fill_slots", 1 << 20)
    return call(in_specs=[WHOLE] * 3, out_specs=[WHOLE] * 2)(hidden, router.T, expert_ids.T)


def route_experts(incoming, places, weights, seen, packed, state, shape):
    model_width = incoming.shape[1]
    exp_count = lax.axis_size("exp")
    rows = lax.all_gather(
        incoming, "ctx", axis=0, tiled=True, axis_index_groups=RINGS
    )
    rows, seen, packed = lax.optimization_barrier((rows, seen, packed))
    listed = trade(packed)
    (partial,) = expert_rows([rows], weights)
    summed_output = lax.psum_scatter(
        partial, "ctx", scatter_dimension=0, tiled=True, axis_index_groups=RINGS
    )
    attention = unpack(trade(attend(state, seen, listed)), shape)
    summed_output, attention = lax.optimization_barrier((summed_output, attention))
    returned = trade(summed_output.reshape(exp_count, -1, model_width))
    moe_out = lax.dot_general(
        places,
        returned.reshape(-1, model_width),
        (((0,), (0,)), ((), ())),
        preferred_element_type=jnp.float32,
    ).astype(jnp.bfloat16)
    return attention, moe_out


def shards(
    queries,
    key_states,
    value_state_rows,
    block_lists,
    hidden,
    router,
    expert_ids,
    w_gate,
    w_up,
    w_down,
):
    own = (w_gate[0], w_up[0], w_down[0])
    other = tuple(lax.ppermute(w, "ctx", CORE_SWAP) for w in own)
    experts, width = router.shape[1], router.shape[0]
    capacity = 2 * hidden.shape[0] // experts
    outgoing, places = fill_slots(hidden, router, expert_ids, experts * capacity)
    paired = pair_rows(key_states, value_state_rows)
    incoming = trade(outgoing.reshape(experts, capacity, width)).reshape(-1, width)
    below, above = [paired], [paired]
    for _ in range(3):
        below.append(up_z(below[-1]))
        above.append(down_z(above[-1]))
    incoming, below[3], above[3] = lax.optimization_barrier(
        (incoming, below[3], above[3])
    )
    seen = trade(pack_own(below[0], queries))
    packed, state = exchange_rows(below, above, block_lists)
    attention, moe_out = route_experts(
        incoming, places, own + other, seen, packed, state, queries.shape
    )
    return (attention, moe_out)


def solution(mesh):
    placed = (
        P(None, ("ctx", "exp"), None),
        P(None, ("ctx", "exp"), None),
        P(None, ("ctx", "exp"), None),
        P(),
        P(("ctx", "exp"), None),
        P(),
        P(("ctx", "exp"), None),
        P("exp", None, "ctx"),
        P("exp", None, "ctx"),
        P("exp", "ctx", None),
    )
    return jax.shard_map(
        shards,
        mesh=mesh,
        in_specs=placed,
        out_specs=(P(None, ("ctx", "exp"), None), P(("ctx", "exp"), None)),
        check_vma=False,
    )
```

```python
import functools

import jax
import jax.numpy as jnp
from jax import lax
from jax.experimental import pallas as pl
from jax.experimental.pallas import tpu as pltpu
from jax.sharding import PartitionSpec as P

HEAD_DIM = 128
NEGATIVE_LARGE = -1e30
SIDE = 4
RINGS = [[2 * z + c for z in range(8)] for c in range(2)]
CORE_SWAP = [(i, i ^ 1) for i in range(16)]


def ordinary(vmem=48):
    return pltpu.CompilerParams(
        dimension_semantics=("arbitrary",), vmem_limit_bytes=vmem * 1024 * 1024
    )


WHOLE = pl.BlockSpec(memory_space=pltpu.VMEM)
TABLE = pl.BlockSpec(memory_space=pltpu.SMEM)


def small(kernel, outs, name, moved, scratch=()):
    return functools.partial(
        pl.pallas_call,
        kernel,
        out_shape=outs,
        scratch_shapes=scratch,
        compiler_params=pltpu.CompilerParams(vmem_limit_bytes=16 * 1024 * 1024),
        cost_estimate=pl.CostEstimate(flops=0, bytes_accessed=moved, transcendentals=0),
        name=name,
    )


def pair_kernel(keys, values, out):
    for h in range(SIDE):
        out[:, :, h * 256 : h * 256 + 128] = keys[:, :, h * 128 : h * 128 + 128]
        out[:, :, h * 256 + 128 : h * 256 + 256] = values[:, :, h * 128 : h * 128 + 128]


def pair_rows(keys, values):
    shape = keys.shape[:2] + (2 * keys.shape[2],)
    call = small(pair_kernel, jax.ShapeDtypeStruct(shape, keys.dtype), "pair_rows", 1 << 19)
    return call(in_specs=[WHOLE] * 2, out_specs=WHOLE)(keys, values)


def ring(d):
    return [(2 * z + c, 2 * ((z + d) % 8) + c) for z in range(8) for c in range(2)]


def up_z(v):
    return lax.ppermute(v, "ctx", ring(1))


def down_z(v):
    return lax.ppermute(v, "ctx", ring(-1))


def choose_kernel(table, *refs):
    own, b1, b2, b3, far_low, far_high, a3, a2, a1, mine, theirs, held = refs
    for k, block in ((0, own), (1, b1), (2, b2), (3, b3), (5, a3), (6, a2), (7, a1)):
        held[2 * k] = block[0]
        held[2 * k + 1] = block[1]
    held[8] = far_low[0]
    held[9] = far_high[0]
    for i in range(2):
        mine[i] = held[table[i]]
        theirs[i] = held[table[2 + i]]


def choose_blocks(below, above, table):
    paired = below[0]
    far_low, far_high = up_z(below[3][:1]), down_z(above[3][1:])
    out = jax.ShapeDtypeStruct(paired.shape, paired.dtype)
    held = pltpu.VMEM((16,) + paired.shape[1:], paired.dtype)
    call = small(choose_kernel, [out, out], "choose_blocks", 3 << 20, [held])
    return call(in_specs=[TABLE] + [WHOLE] * 9, out_specs=[WHOLE] * 2)(
        table, paired, *below[1:], far_low, far_high, above[3], above[2], above[1]
    )


def pack_own_kernel(own, queries, out):
    group = queries.shape[2] // (SIDE * HEAD_DIM)
    for h in range(SIDE):
        at = h * 256
        for y in range(SIDE):
            to = SIDE * h + y
            for b in range(2):
                out[to, b * 128 : b * 128 + 64] = own[b, :, at : at + 128]
                out[to, b * 128 + 64 : b * 128 + 128] = own[b, :, at + 128 : at + 256]
                for g in range(group):
                    row = 256 + (b * group + g) * 16
                    column = (h * group + g) * HEAD_DIM
                    out[to, row : row + 16] = queries[
                        b, 16 * y : 16 * y + 16, column : column + HEAD_DIM
                    ]


def pack_own(own, queries):
    rows = 256 + 2 * 16 * queries.shape[2] // (SIDE * HEAD_DIM)
    out = jax.ShapeDtypeStruct((SIDE * SIDE, rows, HEAD_DIM), own.dtype)
    call = small(pack_own_kernel, out, "pack_own", 3 << 20)
    return call(in_specs=[WHOLE] * 2, out_specs=WHOLE)(own, queries)


def pack_listed_kernel(table, mine, swapped, out):
    for h in range(SIDE):
        at = h * 256
        for b in range(2):
            piece = jnp.where(
                table[b] > 0, mine[b, :, at : at + 256], swapped[b, :, at : at + 256]
            )
            for y in range(SIDE):
                out[SIDE * h + y, b * 128 : b * 128 + 64] = piece[:, :HEAD_DIM]
                out[SIDE * h + y, b * 128 + 64 : b * 128 + 128] = piece[:, HEAD_DIM:]


def pack_listed(table, mine, swapped):
    out = jax.ShapeDtypeStruct((SIDE * SIDE, 256, HEAD_DIM), mine.dtype)
    call = small(pack_listed_kernel, out, "pack_listed", 3 << 20)
    return call(in_specs=[TABLE] + [WHOLE] * 2, out_specs=WHOLE)(table, mine, swapped)


def unpack_kernel(back, out):
    group = out.shape[2] // (SIDE * HEAD_DIM)
    for h in range(SIDE):
        for y in range(SIDE):
            for p in range(2):
                for g in range(group):
                    row = (p * group + g) * 16
                    column = (h * group + g) * HEAD_DIM
                    out[p, 16 * y : 16 * y + 16, column : column + HEAD_DIM] = back[
                        SIDE * h + y, row : row + 16
                    ]


def unpack(back, shape):
    call = small(unpack_kernel, jax.ShapeDtypeStruct(shape, back.dtype), "unpack", 1310720)
    return call(in_specs=[WHOLE], out_specs=WHOLE)(back)


NT = (((1,), (1,)), ((), ()))


def attend_kernel(table, seen, listed, out, kown, vown, klist, vlist):
    p = pl.program_id(0)
    y, usable = table[0], table[1 + p]
    own_at = pl.multiple_of(p * 128, 128)
    for e in range(SIDE * SIDE):
        at = pl.ds(e * 64, 64)
        kown[at, :] = seen[e, pl.ds(own_at, 64), :]
        vown[at, :] = seen[e, pl.ds(own_at + 64, 64), :]
        klist[at, :] = listed[e, pl.ds(own_at, 64), :]
        vlist[at, :] = listed[e, pl.ds(own_at + 64, 64), :]
    scaling = HEAD_DIM ** (-0.5)
    group = out.shape[1] // 32
    rows = 64 * group
    row = lax.rem(lax.broadcasted_iota(jnp.int32, (rows, 256), 0), 64)
    query_pos = lax.div(row, 16) * 64 + 16 * y + lax.rem(row, 16)
    diagonal = lax.broadcasted_iota(jnp.int32, (rows, 256), 1) <= query_pos
    for case in range(SIDE):
        pieces = []
        for g in range(group):
            at = pl.multiple_of(256 + (p * group + g) * 16, 16)
            for e in range(SIDE):
                pieces.append(seen[SIDE * case + e, pl.ds(at, 16), :])
        query = jnp.concatenate(pieces, axis=0)
        before = case * 256
        own = lax.dot_general(
            query, kown[pl.ds(before, 256), :], NT, preferred_element_type=jnp.float32
        )
        own = jnp.where(diagonal, own * scaling, NEGATIVE_LARGE)
        far = lax.dot_general(query, klist[...], NT, preferred_element_type=jnp.float32)
        far = jnp.where(usable > 0, far * scaling, NEGATIVE_LARGE)
        top = jnp.maximum(jnp.max(own, axis=1, keepdims=True), jnp.max(far, axis=1, keepdims=True))
        if case:
            near = lax.dot_general(
                query, kown[pl.ds(0, before), :], NT, preferred_element_type=jnp.float32
            )
            near = near * scaling
            top = jnp.maximum(top, jnp.max(near, axis=1, keepdims=True))
        own = jnp.exp(own - top)
        far = jnp.exp(far - top)
        total = jnp.sum(own, axis=1, keepdims=True) + jnp.sum(far, axis=1, keepdims=True)
        mixed = jnp.dot(
            own.astype(jnp.bfloat16), vown[pl.ds(before, 256), :], preferred_element_type=jnp.float32
        ) + jnp.dot(far.astype(jnp.bfloat16), vlist[...], preferred_element_type=jnp.float32)
        if case:
            near = jnp.exp(near - top)
            total = total + jnp.sum(near, axis=1, keepdims=True)
            mixed = mixed + jnp.dot(
                near.astype(jnp.bfloat16),
                vown[pl.ds(0, before), :],
                preferred_element_type=jnp.float32,
            )
        mixed = (mixed / total).astype(jnp.bfloat16)
        for g in range(group):
            at = pl.multiple_of((p * group + g) * 16, 16)
            for e in range(SIDE):
                start = g * 64 + e * 16
                out[SIDE * case + e, pl.ds(at, 16), :] = mixed[start : start + 16]


def attend(table, seen, listed):
    rows = seen.shape[1] - 256
    out = jax.ShapeDtypeStruct((seen.shape[0], rows, seen.shape[2]), seen.dtype)
    zeros = lambda i, t: (0, 0, 0)
    return pl.pallas_call(
        attend_kernel,
        grid_spec=pltpu.PrefetchScalarGridSpec(
            num_scalar_prefetch=1,
            grid=(2,),
            in_specs=[pl.BlockSpec(seen.shape, zeros), pl.BlockSpec(listed.shape, zeros)],
            out_specs=pl.BlockSpec(out.shape, zeros),
            scratch_shapes=[pltpu.VMEM((1024, HEAD_DIM), jnp.bfloat16)] * 4,
        ),
        out_shape=out,
        compiler_params=ordinary(40),
        cost_estimate=pl.CostEstimate(
            flops=2200000000, bytes_accessed=4 << 20, transcendentals=4300000
        ),
        name="attend",
    )(table, seen, listed)


def exchange_rows(below, above, block_lists):
    ctx_count = lax.axis_size("ctx")
    blocks_total = 2 * ctx_count
    ctx_index = lax.axis_index("ctx")
    exp_index = lax.axis_index("exp")
    y = lax.rem(exp_index, SIDE)
    z, core = lax.div(ctx_index, 2), lax.rem(ctx_index, 2)
    other = ctx_index + 1 - 2 * core
    own_blocks = jnp.stack(
        [ctx_index, blocks_total - 1 - ctx_index, other, blocks_total - 1 - other]
    )
    listed = block_lists[own_blocks]
    usable = (listed != own_blocks).astype(jnp.int32)
    holder = jnp.minimum(listed, blocks_total - 1 - listed)
    distance = lax.rem(z + 8 - lax.div(holder, 2), 8)
    chosen = (2 * distance + (listed >= ctx_count).astype(jnp.int32)).astype(jnp.int32)
    local = (lax.rem(holder, 2) == core).astype(jnp.int32)

    mine, theirs = choose_blocks(below, above, chosen)
    swapped = lax.ppermute(theirs, "ctx", CORE_SWAP)
    packed = pack_listed(local[:2], mine, swapped)
    return packed, jnp.concatenate([y[None], usable[:2]]).astype(jnp.int32)


def trade(v):
    return lax.all_to_all(v, "exp", split_axis=0, concat_axis=0, tiled=True)


def ffn_kernel(counts, refs):
    xs, ws, outs = refs[:counts], refs[counts : counts + 6], refs[counts + 6 : 2 * counts + 6]
    rows, gates, downs, results, act, w_sem, x_sem, o_sem = refs[2 * counts + 6 :]
    width, hidden = gates.shape[1], gates.shape[2] // 2
    step = rows.shape[1]
    parts = []
    for x, out in zip(xs, outs):
        for at in range(0, x.shape[0], step):
            parts.append((x, out, at, min(step, x.shape[0] - at)))
    loads = [
        pltpu.make_async_copy(
            x.at[pl.ds(at, n), :], rows.at[k, pl.ds(0, n), :], x_sem.at[k]
        )
        for k, (x, _, at, n) in enumerate(parts)
    ]
    stores = [
        pltpu.make_async_copy(
            results.at[k, pl.ds(0, n), :], out.at[pl.ds(at, n), :], o_sem.at[k]
        )
        for k, (_, out, at, n) in enumerate(parts)
    ]
    targets = [gates.at[h, :, pl.ds(c * hidden, hidden)] for h in range(2) for c in range(2)]
    targets += [downs.at[pl.ds(0, hidden), :], downs.at[pl.ds(hidden, hidden), :]]
    order = (0, 1, 3, 4, 2, 5)
    weights = [pltpu.make_async_copy(ws[w], targets[k], w_sem.at[k]) for k, w in enumerate(order)]
    loads[0].start()
    for copy in weights:
        copy.start()
    for copy in loads[1:]:
        copy.start()
    block = 2560
    for k, (x, out, at, n) in enumerate(parts):
        loads[k].wait()
        for half in range(2):
            if k == 0:
                weights[2 * half].wait()
                weights[2 * half + 1].wait()
            both = jnp.dot(rows[k, :n], gates[half], preferred_element_type=jnp.float32)
            gate, up = both[:, :hidden], both[:, hidden:]
            act[:n, half * hidden : (half + 1) * hidden] = (
                gate / (1.0 + jnp.exp(-gate)) * up
            ).astype(jnp.bfloat16)
        if k == 0:
            weights[4].wait()
            weights[5].wait()

        @pl.loop(0, width // block)
        def _(c, k=k, n=n):
            columns = pl.ds(pl.multiple_of(c * block, block), block)
            part = jnp.dot(act[:n], downs[:, columns], preferred_element_type=jnp.float32)
            results[k, :n, columns] = part.astype(jnp.bfloat16)

        stores[k].start()
    for copy in stores:
        copy.wait()


def expert_rows(xs, weights, step=256):
    width = xs[0].shape[1]
    hidden = weights[0].shape[1]
    tokens = sum(x.shape[0] for x in xs)
    step = min(step, max(x.shape[0] for x in xs))
    parts = sum(-(-x.shape[0] // step) for x in xs)
    far = pl.BlockSpec(memory_space=pltpu.HBM)
    return pl.pallas_call(
        lambda *refs: ffn_kernel(len(xs), refs),
        in_specs=[far] * (len(xs) + 6),
        out_specs=[far] * len(xs),
        out_shape=[jax.ShapeDtypeStruct(x.shape, jnp.bfloat16) for x in xs],
        scratch_shapes=[
            pltpu.VMEM((parts, step, width), jnp.bfloat16),
            pltpu.VMEM((2, width, 2 * hidden), jnp.bfloat16),
            pltpu.VMEM((2 * hidden, width), jnp.bfloat16),
            pltpu.VMEM((parts, step, width), jnp.bfloat16),
            pltpu.VMEM((step, 2 * hidden), jnp.bfloat16),
            pltpu.SemaphoreType.DMA((6,)),
            pltpu.SemaphoreType.DMA((parts,)),
            pltpu.SemaphoreType.DMA((parts,)),
        ],
        compiler_params=pltpu.CompilerParams(vmem_limit_bytes=60 * 1024 * 1024),
        cost_estimate=pl.CostEstimate(
            flops=12 * tokens * width * hidden,
            bytes_accessed=12 * width * hidden + 4 * tokens * width,
            transcendentals=2 * tokens * hidden,
        ),
        name="expert_rows",
    )(*xs, *weights)


def slot_kernel(hidden, router, ids, out, places):
    experts, tokens, slots = router.shape[0], hidden.shape[0], out.shape[0]
    logits = lax.dot_general(router[...], hidden[...], NT, preferred_element_type=jnp.float32)
    named = ids[...] == lax.broadcasted_iota(jnp.int32, (experts, tokens), 0)
    onehot = jnp.where(named, 1.0, 0.0)
    gate_row = 1.0 / (1.0 + jnp.exp(-jnp.sum(logits * onehot, axis=0, keepdims=True)))
    row = lax.broadcasted_iota(jnp.int32, (tokens, tokens), 0)
    column = lax.broadcasted_iota(jnp.int32, (tokens, tokens), 1)
    upto = jnp.where(row <= column, 1.0, 0.0).astype(jnp.bfloat16)
    counts = jnp.dot(onehot.astype(jnp.bfloat16), upto, preferred_element_type=jnp.float32)
    rank = jnp.sum(counts * onehot, axis=0, keepdims=True) - 1.0
    slot = ids[...] * (slots // experts) + rank.astype(jnp.int32)
    target = lax.broadcasted_iota(jnp.int32, (slots, tokens), 0)
    place = jnp.where(slot == target, 1.0, 0.0).astype(jnp.bfloat16)
    places[...] = place
    gate_score = jnp.sum(jnp.where(row == column, gate_row, 0.0), axis=1, keepdims=True)
    scaled = (hidden[...].astype(jnp.float32) * gate_score).astype(jnp.bfloat16)
    out[...] = jnp.dot(place, scaled, preferred_element_type=jnp.float32).astype(jnp.bfloat16)


def fill_slots(hidden, router, expert_ids, slots):
    tokens, width = hidden.shape
    outs = [
        jax.ShapeDtypeStruct((slots, width), jnp.bfloat16),
        jax.ShapeDtypeStruct((slots, tokens), jnp.bfloat16),
    ]
    call = small(slot_kernel, outs, "fill_slots", 1 << 20)
    return call(in_specs=[WHOLE] * 3, out_specs=[WHOLE] * 2)(hidden, router.T, expert_ids.T)


def route_experts(incoming, places, weights, seen, packed, state, shape):
    model_width = incoming.shape[1]
    exp_count = lax.axis_size("exp")
    rows = lax.all_gather(
        incoming, "ctx", axis=0, tiled=True, axis_index_groups=RINGS
    )
    rows, seen, packed = lax.optimization_barrier((rows, seen, packed))
    listed = trade(packed)
    (partial,) = expert_rows([rows], weights)
    summed_output = lax.psum_scatter(
        partial, "ctx", scatter_dimension=0, tiled=True, axis_index_groups=RINGS
    )
    attention = unpack(trade(attend(state, seen, listed)), shape)
    summed_output, attention = lax.optimization_barrier((summed_output, attention))
    returned = trade(summed_output.reshape(exp_count, -1, model_width))
    moe_out = lax.dot_general(
        places,
        returned.reshape(-1, model_width),
        (((0,), (0,)), ((), ())),
        preferred_element_type=jnp.float32,
    ).astype(jnp.bfloat16)
    return attention, moe_out


def shards(
    queries,
    key_states,
    value_state_rows,
    block_lists,
    hidden,
    router,
    expert_ids,
    w_gate,
    w_up,
    w_down,
):
    own = (w_gate[0], w_up[0], w_down[0])
    other = tuple(lax.ppermute(w, "ctx", CORE_SWAP) for w in own)
    experts, width = router.shape[1], router.shape[0]
    capacity = 2 * hidden.shape[0] // experts
    outgoing, places = fill_slots(hidden, router, expert_ids, experts * capacity)
    paired = pair_rows(key_states, value_state_rows)
    incoming = trade(outgoing.reshape(experts, capacity, width)).reshape(-1, width)
    below, above = [paired], [paired]
    for _ in range(2):
        below.append(up_z(below[-1]))
        above.append(down_z(above[-1]))
    incoming, below[2], above[2] = lax.optimization_barrier(
        (incoming, below[2], above[2])
    )
    for _ in range(1):
        below.append(up_z(below[-1]))
        above.append(down_z(above[-1]))
    seen = trade(pack_own(below[0], queries))
    packed, state = exchange_rows(below, above, block_lists)
    attention, moe_out = route_experts(
        incoming, places, own + other, seen, packed, state, queries.shape
    )
    return (attention, moe_out)


def solution(mesh):
    placed = (
        P(None, ("ctx", "exp"), None),
        P(None, ("ctx", "exp"), None),
        P(None, ("ctx", "exp"), None),
        P(),
        P(("ctx", "exp"), None),
        P(),
        P(("ctx", "exp"), None),
        P("exp", None, "ctx"),
        P("exp", None, "ctx"),
        P("exp", "ctx", None),
    )
    return jax.shard_map(
        shards,
        mesh=mesh,
        in_specs=placed,
        out_specs=(P(None, ("ctx", "exp"), None), P(("ctx", "exp"), None)),
        check_vma=False,
    )
```
